256 devices in a mesh: ctx: 64 (over y, z, core), head: 4 (over x).
Axes of the slice: x: 4, y: 4, z: 8, core: 2. Of those that a mesh axis runs over, the one named last changes fastest.
Arguments:
- queries: bfloat16 [8192, 32, 128], P('ctx', 'head'), may hold values from -70 to 70
- keys: bfloat16 [8192, 32, 128], P('ctx', 'head'), may hold values from -6 to 6
- values: bfloat16 [8192, 32, 128], P('ctx', 'head'), may hold values from -6 to 6
- teacher: bfloat16 [8192, 32, 128], P('ctx', 'head'), may hold values from -18 to 18
- wq: bfloat16 [32, 64, 128], P('head'), may hold values from -0.5 to 0.5
- wk: bfloat16 [32, 64, 128], P('head'), may hold values from -0.5 to 0.5
Outputs:
- student: bfloat16 [8192, 32, 128], P('ctx', 'head')
- loss: float32 [], replicated
- grad_wq: float32 [32, 64, 128], P('head')
- grad_wk: float32 [32, 64, 128], P('head')
The draws below stay inside these ranges and needn't reach their ends.
All inputs are finite; a program needn't handle non-finite values.
Results may differ from the reference program's by a relative error of at most 0.006.
Values may be sent and summed in bfloat16 or wider, within the bound.
A program may use at most 128 MiB of HBM per device.

```python
import jax
import jax.numpy as jnp
from jax import lax

HEADS = 32
HD = 128
HF = 64
FEAT = 128
WIN = 64
TOK_DEV = 128
TOKENS = 8192


def draw_queries(key, part):
    base = jnp.clip(jax.random.normal(key, (TOKENS, HEADS, HD), jnp.float32), -6.0, 6.0)
    return base.astype(jnp.bfloat16)


def draw_teacher(key, part):
    place = jnp.arange(TOKENS, dtype=jnp.float32) / max(TOKENS - 1, 1)
    base = jnp.clip(jax.random.normal(key, (TOKENS, HEADS, HD), jnp.float32), -6.0, 6.0)
    return (base * (1.0 + 2.0 * place)[:, None, None]).astype(jnp.bfloat16)


def block_scale(stream_key, extent, pieces, low, largest):
    factor_of, own = 1.0, jax.random.fold_in(stream_key, 6)
    for position, parts in pieces:
        steps = jnp.exp(jax.random.uniform(jax.random.fold_in(own, position), (parts,), jnp.float32, low / len(pieces), largest / len(pieces)))
        factor_of = factor_of * jnp.repeat(steps, extent[position] // parts).reshape([-1 if axis == position else 1 for axis in range(len(extent))])
    return factor_of


def noise(stream_key, extent, deviation, reach, split=(), kind=jnp.bfloat16):
    array = jax.random.normal(stream_key, extent, jnp.float32) * deviation
    if len(split) > 0:
        array = block_scale(stream_key, extent, split, -0.22, 0.18) * array
    return jnp.clip(array, min=-reach, max=reach).astype(kind)


def setup_inputs(seed: int = 0) -> dict:
    streams_of = jax.random.split(jax.random.key(seed), 7)
    return {
        "queries": draw_queries(jax.random.fold_in(streams_of[6], 71), 0),
        "keys": noise(streams_of[1], (TOKENS, HEADS, HD), 1.0, 6.0, ((0, 64), (1, 4))),
        "values": noise(streams_of[2], (TOKENS, HEADS, HD), 1.0, 6.0, ((0, 64), (1, 4))),
        "teacher": draw_teacher(jax.random.fold_in(streams_of[6], 71), 0),
        "wq": noise(streams_of[4], (HEADS, HF, HD), HD ** -0.5, 0.5, ((0, 4),)),
        "wk": noise(streams_of[5], (HEADS, HF, HD), HD ** -0.5, 0.5, ((0, 4),)),
    }


def phi(x, w):
    proj = jnp.einsum('thd,hfd->thf', x.astype(jnp.float32), w, precision=lax.Precision.HIGHEST)
    return jnp.concatenate([jax.nn.softmax(proj, axis=-1), jax.nn.softmax(-proj, axis=-1)], axis=-1)

def reference(queries, keys, values, teacher, wq, wk):
    nblock = TOKENS // TOK_DEV
    high = lax.Precision.HIGHEST
    scale = 1.0 / HD ** 0.5
    key_pad = jnp.concatenate([jnp.zeros((WIN, HEADS, HD), jnp.bfloat16), keys], axis=0)
    val_pad = jnp.concatenate([jnp.zeros((WIN, HEADS, HD), jnp.bfloat16), values], axis=0)
    rows = jnp.arange(TOK_DEV, dtype=jnp.int32)[:, None]
    cols = jnp.arange(WIN + TOK_DEV, dtype=jnp.int32)[None, :]
    lower = cols[:, :TOK_DEV] <= rows

    def forward(wq_f, wk_f):

        def step(carry, block):
            state, norm = carry
            first = (block * TOK_DEV).astype(jnp.int32)
            q_blk = lax.dynamic_slice_in_dim(queries, first, TOK_DEV, 0)
            k_blk = lax.dynamic_slice_in_dim(key_pad, first, WIN + TOK_DEV, 0)
            v_blk = lax.dynamic_slice_in_dim(val_pad, first, WIN + TOK_DEV, 0).astype(jnp.float32)
            pos = first - WIN + jnp.arange(WIN + TOK_DEV, dtype=jnp.int32)
            valid = pos >= 0
            early = first + jnp.arange(TOK_DEV, dtype=jnp.int32) < WIN
            inwin = (cols > rows) & (cols <= rows + WIN) & valid[None, :]
            score = jnp.einsum('ihd,chd->hic', q_blk.astype(jnp.float32), k_blk.astype(jnp.float32), precision=high) * scale
            score = jnp.where(inwin[None], score, -jnp.inf)
            top = lax.optimization_barrier(jnp.max(score, axis=-1))
            weight = jnp.where(inwin[None], jnp.exp(score - top[..., None]), 0.0)
            win_num = jnp.einsum('hic,chd->ihd', weight, v_blk, precision=high)
            win_den = lax.optimization_barrier(jnp.sum(weight, axis=-1)).T
            fq = phi(q_blk, wq_f)
            fk = phi(k_blk[:TOK_DEV], wk_f) * valid[:TOK_DEV, None, None].astype(jnp.float32)
            amat = jnp.where(lower[None], jnp.einsum('ihf,chf->hic', fq, fk, precision=high), 0.0)
            lin_num = jnp.einsum('hic,chd->ihd', amat, v_blk[:TOK_DEV], precision=high) + jnp.einsum('ihf,hfd->ihd', fq, state, precision=high)
            lin_den = lax.optimization_barrier(jnp.sum(amat, axis=-1)).T + jnp.einsum('ihf,hf->ih', fq, norm, precision=high)
            top_t = top.T
            win_scale = jnp.where(early[:, None], 1.0, jnp.exp(jnp.minimum(top_t, 0.0)))
            lin_scale = jnp.where(early[:, None], 0.0, jnp.exp(-jnp.maximum(top_t, 0.0)))
            numer = win_scale[..., None] * win_num + lin_scale[..., None] * lin_num
            denom = win_scale * win_den + lin_scale * lin_den
            out = numer / denom[..., None]
            state = state + jnp.einsum('chf,chd->hfd', fk, v_blk[:TOK_DEV], precision=high)
            norm = norm + lax.optimization_barrier(jnp.sum(fk, axis=0))
            return ((state, norm), out)
        init = (jnp.zeros((HEADS, FEAT, HD), jnp.float32), jnp.zeros((HEADS, FEAT), jnp.float32))
        _, outs = lax.scan(step, init, jnp.arange(nblock, dtype=jnp.int32))
        return outs.reshape(TOKENS, HEADS, HD)
    out, pull = jax.vjp(forward, wq.astype(jnp.float32), wk.astype(jnp.float32))
    diff = out - teacher.astype(jnp.float32)
    grad_q, grad_k = pull(2.0 * diff / HD)
    loss = jnp.sum(diff * diff) / (TOKENS * HEADS * HD)
    return (out.astype(jnp.bfloat16), loss, grad_q, grad_k)
```

```python
import jax
import jax.numpy as jnp
from jax import lax
from jax.experimental import pallas as pl
from jax.experimental.pallas import tpu as pltpu
from jax.sharding import PartitionSpec as P

NB = 8
CH = 128
WIN = 64
HD = 128
HF = 64
AUG = 144
FAR = (4, 3, 5, 2, 6, 1, 7, 0)
MESH = pl.DeviceIdType.MESH
BF = jnp.bfloat16
F32 = jnp.float32


def nt(a, b):
    return lax.dot_general(a, b, (((1,), (1,)), ((), ())), preferred_element_type=F32)


def nn(a, b):
    return jnp.dot(a, b, preferred_element_type=F32)


def halves(proj):
    e = []
    for s in (proj[:HF], proj[HF:]):
        w = jnp.exp(s - jnp.max(s, axis=0, keepdims=True))
        e.append(w * (1.0 / jnp.sum(w, axis=0, keepdims=True)))
    return jnp.concatenate(e, axis=0)


def proj_grad(feat, grad):
    d = []
    for a in (0, HF):
        u, g = feat[a : a + HF], grad[a : a + HF]
        d.append(u * (g - jnp.sum(u * g, axis=0, keepdims=True)))
    return (d[0] - d[1]).astype(BF)


def split(x):
    norm = x[HD : HD + 1]
    high = norm.astype(BF).astype(F32)
    row = lax.broadcasted_iota(jnp.int32, (AUG - HD, CH), 0)
    aug = jnp.where(row == 0, high, jnp.where(row == 1, norm - high, 0.0))
    return jnp.concatenate([x[:HD], aug], axis=0).astype(BF)


def joined(x):
    return jnp.concatenate([x[:HD], x[HD : HD + 8] + pltpu.roll(x[HD : HD + 8], 7, 0), x[HD + 8 :]], axis=0)


def place(block, head):
    return 16 * (block // 2) + 2 * head + lax.rem(block, 2)


def each(body):
    for n in range(NB):
        body(n)


def kernel(
    q_in, k_in, v_in, t_in, wq_ref, wk_ref,
    stu_out, gq_out, gk_out, loss_out,
    kbuf, vbuf, qbuf, tbuf, fkt, fkb, fqt, fqb, vta, pre, tot, win, lin, gna, gfk, later,
    own1, ag1, own2, ag2, stu, rs_own, rs_got, fin, la, lb, lc, scal,
    x_send, x_recv, h_send, h_recv, a1_send, a1_recv, a2_send, a2_recv,
    s_send, s_recv, r_send, r_recv, f_send, f_recv, l_send, l_recv,
):
    me = lax.axis_index("ctx")
    xme = lax.axis_index("head")
    src_b, src_j = me // NB, lax.rem(me, NB)
    b = 2 * (me // 16) + lax.rem(me, 2)
    h = lax.rem(me, 16) // 2
    first_block = b == 0

    def ctx(i):
        return {"ctx": i}

    bar = pltpu.get_barrier_semaphore()

    def greet(o, _):
        pl.semaphore_signal(bar, inc=1, device_id=ctx(lax.rem(me + o, 64)), device_id_type=MESH)
        return 0

    lax.fori_loop(1, 64, greet, 0)
    for o in range(1, 4):
        pl.semaphore_signal(bar, inc=1, device_id={"head": lax.rem(xme + o, 4)}, device_id_type=MESH)
    pl.semaphore_wait(bar, 66)

    arrays = ((k_in, kbuf, WIN), (v_in, vbuf, WIN), (q_in, qbuf, 0), (t_in, tbuf, 0))

    def exchange(a, o, act):
        src, dst, base = arrays[a]
        hd = lax.rem(h + o, NB)
        to = place(src_b, hd)
        rows = dst.at[pl.ds(pl.multiple_of(base + CH * src_j, WIN), CH)]

        def remote():
            act(pltpu.make_async_remote_copy(
                src.at[hd], rows, x_send.at[a, o], x_recv.at[a], device_id=ctx(to), device_id_type=MESH))

        if o == 0:
            pl.when(to != me)(remote)
            if act is go:
                @pl.when(to == me)
                def _():
                    pltpu.make_async_copy(src.at[hd], rows, x_recv.at[a]).start()
        else:
            remote()

    def go(c):
        c.start()

    def sent(c):
        c.wait_send()

    tail = jnp.logical_and(src_j == NB - 1, src_b < NB - 1)

    def halo(a, o, act):
        src, dst, _ = arrays[a]
        hd = lax.rem(h + o, NB)
        to = place(src_b + 1, hd)

        def remote():
            act(pltpu.make_async_remote_copy(
                src.at[hd, pl.ds(CH - WIN, WIN)], dst.at[pl.ds(0, WIN)], h_send.at[a, o], h_recv.at[a],
                device_id=ctx(to), device_id_type=MESH))

        if o == 0:
            pl.when(to != me)(remote)
            if act is go:
                @pl.when(to == me)
                def _():
                    pltpu.make_async_copy(
                        src.at[hd, pl.ds(CH - WIN, WIN)], dst.at[pl.ds(0, WIN)], h_recv.at[a]).start()
        else:
            remote()

    for o in FAR:
        exchange(0, o, go)
        exchange(1, o, go)

    @pl.when(tail)
    def _():
        for o in FAR:
            halo(0, o, go)
            halo(1, o, go)

    for a in (2, 3):
        for o in FAR:
            exchange(a, o, go)

    @pl.when(first_block)
    def _():
        kbuf[pl.ds(0, WIN)] = jnp.zeros((WIN, HD), BF)
        vbuf[pl.ds(0, WIN)] = jnp.zeros((WIN, HD), BF)

    eye = jnp.where(
        lax.broadcasted_iota(jnp.int32, (CH, CH), 0) == lax.broadcasted_iota(jnp.int32, (CH, CH), 1),
        1.0, 0.0).astype(BF)
    one_row = jnp.where(lax.broadcasted_iota(jnp.int32, (AUG - HD, CH), 0) < 2, 1.0, 0.0)
    wq1, wk1 = wq_ref[h], wk_ref[h]
    w2q = jnp.concatenate([wq1, -wq1], axis=0)
    w2k = jnp.concatenate([wk1, -wk1], axis=0)

    def arrived(a):
        src, dst, base = arrays[a]
        part = dst.at[pl.ds(base, NB * CH)]
        pltpu.make_async_copy(part, part, x_recv.at[a]).wait()

    def halo_arrived(a):
        dst = arrays[a][1]
        part = dst.at[pl.ds(0, WIN)]
        pltpu.make_async_copy(part, part, h_recv.at[a]).wait()

    arrived(0)
    arrived(1)

    @pl.when(b > 0)
    def _():
        halo_arrived(0)
        halo_arrived(1)

    cidx = lax.broadcasted_iota(jnp.int32, (CH, CH), 0)
    iidx = lax.broadcasted_iota(jnp.int32, (CH, CH), 1)
    lower = cidx <= iidx

    tot[...] = jnp.zeros((AUG, CH), F32)

    def key_chunk(n):
        f = halves(nt(w2k, kbuf[pl.ds(n * CH, CH)]))
        if n == 0:
            bad = jnp.logical_and(first_block, iidx < WIN)
            f = jnp.where(bad, 0.0, f)
        fkt[n] = f
        fb = f.astype(BF)
        fk = nt(eye, fb).astype(BF)
        fkb[n] = fk
        va = jnp.concatenate([nt(eye, vbuf[pl.ds(n * CH, CH)]), one_row], axis=0).astype(BF)
        vta[n] = va
        pre[n] = tot[...]
        tot[...] += nn(va, fk)

    each(key_chunk)
    vta[NB, :, pl.ds(0, WIN)] = jnp.concatenate(
        [nt(eye, vbuf[pl.ds(NB * CH, WIN)]), one_row[:, :WIN]], axis=0).astype(BF)
    own1[...] = split(tot[...])

    def scan_copy(o, own, got, send, recv):
        return pltpu.make_async_remote_copy(
            own, got.at[b], send.at[o], recv.at[b], device_id=ctx(place(lax.rem(b + o, NB), h)),
            device_id_type=MESH)

    def forward(o, act):
        @pl.when(b + o < NB)
        def _():
            act(scan_copy(o, own1, ag1, a1_send, a1_recv))

    def backward(o, act):
        @pl.when(b - o >= 0)
        def _():
            act(scan_copy(NB - o, own2, ag2, a2_send, a2_recv))

    for o in range(7, 0, -1):
        forward(o, go)

    arrived(2)
    scale = 1.0 / HD**0.5

    def query_chunk(n):
        q = qbuf[pl.ds(n * CH, CH)]
        f = halves(nt(w2q, q))
        fqt[n] = f
        fb = f.astype(BF)
        fqb[n] = fb
        sc = nt(kbuf[pl.ds(n * CH, CH + WIN)], q) * scale
        ci = lax.broadcasted_iota(jnp.int32, (CH + WIN, CH), 0)
        ii = lax.broadcasted_iota(jnp.int32, (CH + WIN, CH), 1)
        inwin = jnp.logical_and(ci > ii, ci <= ii + WIN)
        if n == 0:
            inwin = jnp.logical_and(inwin, jnp.logical_or(ci >= WIN, b > 0))
        sc = jnp.where(inwin, sc, -jnp.inf)
        top = jnp.max(sc, axis=0, keepdims=True)
        w = jnp.exp(sc - top).astype(BF)
        wn = nn(vta[n], w[:CH]) + nn(vta[n + 1, :, pl.ds(0, WIN)], w[CH:])
        ws = jnp.exp(jnp.minimum(top, 0.0))
        ls = jnp.exp(-jnp.maximum(top, 0.0))
        if n == 0:
            early = jnp.logical_and(first_block, lax.broadcasted_iota(jnp.int32, (1, CH), 1) < WIN)
            ws = jnp.where(early, 1.0, ws)
            ls = jnp.where(early, 0.0, ls)
        am = jnp.where(lower, nn(fkb[n], fb), 0.0).astype(BF)
        ln = nn(vta[n], am) + nn(split(pre[n]), fb)
        win[n] = ws * wn + ls * ln
        scal[n] = jnp.broadcast_to(ls, (8, CH))

    each(query_chunk)

    lin[...] = jnp.zeros((AUG, CH), F32)
    for m in range(NB - 1):
        @pl.when(m < b)
        def _():
            pltpu.make_async_copy(ag1.at[m], ag1.at[m], a1_recv.at[m]).wait()
            lin[...] += ag1[m].astype(F32)
    carry = joined(lin[...])
    carry_b = split(carry)
    arrived(3)

    la[b] = jnp.zeros((8, CH), F32)
    later[NB - 1] = jnp.zeros((AUG, CH), F32)

    def out_chunk(k):
        n = NB - 1 - k
        ls = scal[n][:1]
        full = win[n] + ls * nn(carry_b, fqb[n])
        inv = 1.0 / full[HD : HD + 1]
        out = full[:HD] * inv
        stu[n] = nt(eye, out.astype(BF)).astype(BF)
        diff = out - nt(eye, tbuf[pl.ds(n * CH, CH)])
        sq = diff * diff
        acc = sq[0:8]
        for r in range(1, HD // 8):
            acc = acc + sq[8 * r : 8 * r + 8]
        la[b] += acc
        coef = ls * inv
        g = diff * (2.0 / HD)
        gd = -coef * jnp.sum(g * out, axis=0, keepdims=True)
        scal[n] = jnp.broadcast_to(gd, (8, CH))
        ga = jnp.concatenate([coef * g, gd * one_row], axis=0).astype(BF)
        gna[n] = ga
        step = nt(ga, fqb[n])
        if n > 0:
            later[n - 1] = later[n] + step
        else:
            own2[...] = split(later[0] + step)

    each(out_chunk)
    for o in range(7, 0, -1):
        backward(o, go)

    def student(j, act):
        to = NB * b + j

        def remote():
            act(pltpu.make_async_remote_copy(
                stu.at[j], stu_out.at[h], s_send.at[j], s_recv, device_id=ctx(to), device_id_type=MESH))

        pl.when(to != me)(remote)
        if act is go:
            @pl.when(to == me)
            def _():
                pltpu.make_async_copy(stu.at[j], stu_out.at[h], s_recv).start()

    for j in range(NB):
        student(j, go)

    def loss_a(o, act):
        act(pltpu.make_async_remote_copy(
            la.at[b], la.at[b], l_send.at[0, o], l_recv.at[0],
            device_id=ctx(place(lax.rem(b + o, NB), h)), device_id_type=MESH))

    def loss_b(o, act):
        act(pltpu.make_async_remote_copy(
            lb.at[xme], lb.at[xme], l_send.at[1, o], l_recv.at[1],
            device_id={"head": lax.rem(xme + o, 4)}, device_id_type=MESH))

    def loss_c(o, act):
        act(pltpu.make_async_remote_copy(
            lc.at[h], lc.at[h], l_send.at[2, o], l_recv.at[2],
            device_id=ctx(place(b, lax.rem(h + o, NB))), device_id_type=MESH))

    def total(ref, count, level):
        part = ref.at[pl.ds(0, count - 1)]
        pltpu.make_async_copy(part, part, l_recv.at[level]).wait()
        acc = ref[0]
        for m in range(1, count):
            acc = acc + ref[m]
        return acc

    for o in range(1, NB):
        loss_a(o, go)

    dq = []

    def mix_chunk(n):
        gd = scal[n][:1]
        ga = gna[n]
        mx = nn(vbuf[pl.ds(n * CH, CH)], ga[:HD]) + gd
        mx = jnp.where(lower, mx, 0.0).astype(BF)
        st = nt(eye, split(pre[n] + carry)).astype(BF)
        gq = nn(fkt[n].astype(BF), mx) + nn(st, ga)
        dq.append(proj_grad(fqt[n], gq))
        lt = nt(eye, split(later[n])).astype(BF)
        gfk[n] = nt(fqb[n], mx) + nn(lt, vta[n])

    each(mix_chunk)
    grad_q = nn(jnp.concatenate(dq, axis=1), qbuf[...])
    rs_own[pl.ds(0, HF)] = grad_q.astype(BF)

    lb[xme] = total(la, NB, 0)
    for o in range(1, 4):
        loss_b(o, go)

    lin[...] = jnp.zeros((AUG, CH), F32)
    for m in range(1, NB):
        @pl.when(m > b)
        def _():
            pltpu.make_async_copy(ag2.at[m], ag2.at[m], a2_recv.at[m]).wait()
            lin[...] += ag2[m].astype(F32)
    after = nt(eye, split(joined(lin[...]))).astype(BF)
    dk = []

    def key_grad(n):
        dk.append(proj_grad(fkt[n], gfk[n] + nn(after, vta[n])))

    each(key_grad)
    grad_k = nn(jnp.concatenate(dk, axis=1), kbuf[pl.ds(0, NB * CH)])
    rs_own[pl.ds(HF, HF)] = grad_k.astype(BF)

    def reduce(o, act):
        m = lax.rem(b + o, NB)
        act(pltpu.make_async_remote_copy(
            rs_own.at[pl.ds(pl.multiple_of(16 * m, 16), 16)], rs_got.at[b], r_send.at[o], r_recv,
            device_id=ctx(place(m, h)), device_id_type=MESH))

    for o in range(1, NB):
        reduce(o, go)
    rs_got[b] = rs_own[pl.ds(pl.multiple_of(16 * b, 16), 16)]
    lc[h] = total(lb, 4, 1)
    for o in range(1, NB):
        loss_c(o, go)
    part = rs_got.at[pl.ds(0, NB - 1)]
    pltpu.make_async_copy(part, part, r_recv).wait()
    acc = rs_got[0].astype(F32)
    for m in range(1, NB):
        acc = acc + rs_got[m].astype(F32)
    slot = NB * h + b
    fin[slot] = acc.astype(BF)

    def spread(o, _):
        pltpu.make_async_remote_copy(
            fin.at[slot], fin.at[slot], f_send, f_recv,
            device_id=ctx(lax.rem(me + o, 64)), device_id_type=MESH).start()
        return 0

    lax.fori_loop(1, 64, spread, 0)

    loss_out[...] = total(lc, NB, 2)

    for o in range(NB):
        for a in range(4):
            exchange(a, o, sent)

    @pl.when(tail)
    def _():
        for o in range(NB):
            halo(0, o, sent)
            halo(1, o, sent)

    for o in range(1, NB):
        forward(o, sent)
        backward(o, sent)
        loss_a(o, sent)
        loss_c(o, sent)
        reduce(o, sent)
    for o in range(1, 4):
        loss_b(o, sent)
    for j in range(NB):
        student(j, sent)
    pltpu.make_async_copy(stu_out, stu_out, s_recv).wait()
    part = fin.at[pl.ds(0, 63)]
    pltpu.make_async_copy(part, part, f_send).wait()
    pltpu.make_async_copy(part, part, f_recv).wait()
    for d in range(NB):
        for m in range(4):
            gq_out[d, pl.ds(16 * m, 16)] = fin[NB * d + m].astype(F32)
            gk_out[d, pl.ds(16 * m, 16)] = fin[NB * d + 4 + m].astype(F32)


def per_device(queries, keys, values, teacher, wq, wk):
    heads = [jnp.swapaxes(x, 0, 1) for x in (queries, keys, values, teacher)]
    vm = pl.BlockSpec(memory_space=pltpu.VMEM)
    hbm = pl.BlockSpec(memory_space=pl.ANY)
    dma = pltpu.SemaphoreType.DMA
    stu, gq, gk, loss = pl.pallas_call(
        kernel,
        out_shape=(
            jax.ShapeDtypeStruct((NB, CH, HD), BF),
            jax.ShapeDtypeStruct((NB, HF, HD), F32),
            jax.ShapeDtypeStruct((NB, HF, HD), F32),
            jax.ShapeDtypeStruct((8, CH), F32),
        ),
        in_specs=[hbm] * 4 + [vm] * 2,
        out_specs=(vm, vm, vm, vm),
        scratch_shapes=[
            pltpu.VMEM((NB * CH + WIN, HD), BF),
            pltpu.VMEM((NB * CH + WIN, HD), BF),
            pltpu.VMEM((NB * CH, HD), BF),
            pltpu.VMEM((NB * CH, HD), BF),
            pltpu.VMEM((NB, CH, CH), F32),
            pltpu.VMEM((NB, CH, CH), BF),
            pltpu.VMEM((NB, CH, CH), F32),
            pltpu.VMEM((NB, CH, CH), BF),
            pltpu.VMEM((NB + 1, AUG, CH), BF),
            pltpu.VMEM((NB, AUG, CH), F32),
            pltpu.VMEM((AUG, CH), F32),
            pltpu.VMEM((NB, AUG, CH), F32),
            pltpu.VMEM((AUG, CH), F32),
            pltpu.VMEM((NB, AUG, CH), BF),
            pltpu.VMEM((NB, CH, CH), F32),
            pltpu.VMEM((NB, AUG, CH), F32),
            pltpu.VMEM((AUG, CH), BF),
            pltpu.VMEM((NB, AUG, CH), BF),
            pltpu.VMEM((AUG, CH), BF),
            pltpu.VMEM((NB, AUG, CH), BF),
            pltpu.VMEM((NB, CH, HD), BF),
            pltpu.VMEM((2 * HF, HD), BF),
            pltpu.VMEM((NB, 16, HD), BF),
            pltpu.VMEM((NB * NB, 16, HD), BF),
            pltpu.VMEM((NB, 8, CH), F32),
            pltpu.VMEM((4, 8, CH), F32),
            pltpu.VMEM((NB, 8, CH), F32),
            pltpu.VMEM((NB, 8, CH), F32),
            dma((4, NB)), dma((4,)),
            dma((2, NB)), dma((2,)),
            dma((NB,)), dma((NB,)),
            dma((NB,)), dma((NB,)),
            dma((NB,)), dma,
            dma((NB,)), dma,
            dma, dma,
            dma((3, NB)), dma((3,)),
        ],
        compiler_params=pltpu.CompilerParams(collective_id=0, has_side_effects=True),
    )(*heads, wq, wk)
    entries = 8192 * 32 * 128
    return jnp.swapaxes(stu, 0, 1), jnp.sum(loss) / entries, gq, gk


def solution(mesh):
    tok = P("ctx", "head", None)
    par = P("head", None, None)
    return jax.shard_map(
        per_device,
        mesh=mesh,
        in_specs=(tok, tok, tok, tok, par, par),
        out_specs=(tok, P(), par, par),
        check_vma=False,
    )
```

```python
import jax
import jax.numpy as jnp
from jax import lax
from jax.experimental import pallas as pl
from jax.experimental.pallas import tpu as pltpu
from jax.sharding import PartitionSpec as P

NB = 8
CH = 128
WIN = 64
HD = 128
HF = 64
AUG = 144
FAR = (4, 3, 5, 2, 6, 1, 7, 0)
MESH = pl.DeviceIdType.MESH
BF = jnp.bfloat16
F32 = jnp.float32


def nt(a, b):
    return lax.dot_general(a, b, (((1,), (1,)), ((), ())), preferred_element_type=F32)


def nn(a, b):
    return jnp.dot(a, b, preferred_element_type=F32)


def halves(proj):
    e = []
    for s in (proj[:HF], proj[HF:]):
        w = jnp.exp(s - jnp.max(s, axis=0, keepdims=True))
        e.append(w * (1.0 / jnp.sum(w, axis=0, keepdims=True)))
    return jnp.concatenate(e, axis=0)


def proj_grad(feat, grad):
    d = []
    for a in (0, HF):
        u, g = feat[a : a + HF], grad[a : a + HF]
        d.append(u * (g - jnp.sum(u * g, axis=0, keepdims=True)))
    return (d[0] - d[1]).astype(BF)


def split(x):
    norm = x[HD : HD + 1]
    high = norm.astype(BF).astype(F32)
    row = lax.broadcasted_iota(jnp.int32, (AUG - HD, CH), 0)
    aug = jnp.where(row == 0, high, jnp.where(row == 1, norm - high, 0.0))
    return jnp.concatenate([x[:HD], aug], axis=0).astype(BF)


def joined(x):
    return jnp.concatenate([x[:HD], x[HD : HD + 8] + pltpu.roll(x[HD : HD + 8], 7, 0), x[HD + 8 :]], axis=0)


def place(block, head):
    return 16 * (block // 2) + 2 * head + lax.rem(block, 2)


def each(body):
    for n in range(NB):
        body(n)


def kernel(
    q_hbm, k_hbm, v_hbm, t_hbm, wq_hbm, wk_hbm,
    stu_out, fin_out, loss_out,
    xin, xs, wq_ref, wk_ref,
    kbuf, vbuf, qbuf, tbuf, fkt, fkb, fqt, fqb, vta, pre, tot, win, outs, lin, gna, gfk, later,
    own1, ag1, own2, ag2, stu, stu_got, stu_t, rs_own, rs_got, fin, la, lb, lc, scal,
    in_sem, w_sem, out_sem,
    x_send, x_recv, h_send, h_recv, a1_send, a1_recv, a2_send, a2_recv,
    s_send, s_recv, r_send, r_recv, f_send, f_recv, l_send, l_recv,
):
    me = lax.axis_index("ctx")
    xme = lax.axis_index("head")
    src_b, src_j = me // NB, lax.rem(me, NB)
    b = 2 * (me // 16) + lax.rem(me, 2)
    h = lax.rem(me, 16) // 2
    first_block = b == 0

    def ctx(i):
        return {"ctx": i}

    y, z, c = me // 16, h, lax.rem(me, 2)
    k_in, v_in, q_in, t_in = (xs.at[a] for a in range(4))
    loads = [pltpu.make_async_copy(src, xin.at[a], in_sem.at[a]) for a, src in enumerate((k_hbm, v_hbm, q_hbm, t_hbm))]
    weights = [
        pltpu.make_async_copy(wq_hbm, wq_ref, w_sem.at[0]),
        pltpu.make_async_copy(wk_hbm, wk_ref, w_sem.at[1]),
    ]
    for load in loads + weights:
        load.start()

    bar = pltpu.get_barrier_semaphore()

    def greet(device):
        pl.semaphore_signal(bar, inc=1, device_id=device, device_id_type=MESH)

    for o in FAR:
        for d in range(2):
            if o or d:
                greet(ctx(16 * y + 2 * lax.rem(z + o, NB) + lax.rem(c + d, 2)))
    for o in range(1, 4):
        for d in range(2):
            greet(ctx(16 * lax.rem(y + o, 4) + 2 * z + d))
        greet({"head": lax.rem(xme + o, 4)})
    gives = jnp.logical_and(lax.rem(me, 16) == 15, y < 3)
    takes = jnp.logical_and(c == 0, y > 0)

    @pl.when(gives)
    def _():
        for o in range(NB):
            greet(ctx(16 * (y + 1) + 2 * o))

    @pl.when(takes)
    def _():
        greet(ctx(16 * (y - 1) + 15))

    for a in range(4):
        loads[a].wait()
        xs[a] = jnp.swapaxes(xin[a], 0, 1)
    for load in weights:
        load.wait()
    pl.semaphore_wait(bar, 24 + 8 * gives.astype(jnp.int32) + takes.astype(jnp.int32))

    arrays = ((k_in, kbuf, WIN), (v_in, vbuf, WIN), (q_in, qbuf, 0), (t_in, tbuf, 0))

    def exchange(a, o, act):
        src, dst, base = arrays[a]
        hd = lax.rem(h + o, NB)
        to = place(src_b, hd)
        rows = dst.at[pl.ds(pl.multiple_of(base + CH * src_j, WIN), CH)]

        def remote():
            act(pltpu.make_async_remote_copy(
                src.at[hd], rows, x_send.at[a, o], x_recv.at[a], device_id=ctx(to), device_id_type=MESH))

        if o == 0:
            pl.when(to != me)(remote)
            if act is go:
                @pl.when(to == me)
                def _():
                    pltpu.make_async_copy(src.at[hd], rows, x_recv.at[a]).start()
        else:
            remote()

    def go(c):
        c.start()

    def sent(c):
        c.wait_send()

    tail = jnp.logical_and(src_j == NB - 1, src_b < NB - 1)

    def halo(a, o, act):
        src, dst, _ = arrays[a]
        hd = lax.rem(h + o, NB)
        to = place(src_b + 1, hd)

        def remote():
            act(pltpu.make_async_remote_copy(
                src.at[hd, pl.ds(CH - WIN, WIN)], dst.at[pl.ds(0, WIN)], h_send.at[a, o], h_recv.at[a],
                device_id=ctx(to), device_id_type=MESH))

        if o == 0:
            pl.when(to != me)(remote)
            if act is go:
                @pl.when(to == me)
                def _():
                    pltpu.make_async_copy(
                        src.at[hd, pl.ds(CH - WIN, WIN)], dst.at[pl.ds(0, WIN)], h_recv.at[a]).start()
        else:
            remote()

    for o in FAR:
        exchange(0, o, go)
        exchange(1, o, go)

    @pl.when(tail)
    def _():
        for o in FAR:
            halo(0, o, go)
            halo(1, o, go)

    for a in (2, 3):
        for o in FAR:
            exchange(a, o, go)

    @pl.when(first_block)
    def _():
        kbuf[pl.ds(0, WIN)] = jnp.zeros((WIN, HD), BF)
        vbuf[pl.ds(0, WIN)] = jnp.zeros((WIN, HD), BF)

    eye = jnp.where(
        lax.broadcasted_iota(jnp.int32, (CH, CH), 0) == lax.broadcasted_iota(jnp.int32, (CH, CH), 1),
        1.0, 0.0).astype(BF)
    one_row = jnp.where(lax.broadcasted_iota(jnp.int32, (AUG - HD, CH), 0) < 2, 1.0, 0.0)
    wq1, wk1 = wq_ref[h], wk_ref[h]
    w2q = jnp.concatenate([wq1, -wq1], axis=0)
    w2k = jnp.concatenate([wk1, -wk1], axis=0)

    def arrived(a):
        src, dst, base = arrays[a]
        part = dst.at[pl.ds(base, NB * CH)]
        pltpu.make_async_copy(part, part, x_recv.at[a]).wait()

    def halo_arrived(a):
        dst = arrays[a][1]
        part = dst.at[pl.ds(0, WIN)]
        pltpu.make_async_copy(part, part, h_recv.at[a]).wait()

    arrived(0)
    arrived(1)

    @pl.when(b > 0)
    def _():
        halo_arrived(0)
        halo_arrived(1)

    cidx = lax.broadcasted_iota(jnp.int32, (CH, CH), 0)
    iidx = lax.broadcasted_iota(jnp.int32, (CH, CH), 1)
    lower = cidx <= iidx

    tot[...] = jnp.zeros((AUG, CH), F32)

    def key_chunk(n):
        f = halves(nt(w2k, kbuf[pl.ds(n * CH, CH)]))
        if n == 0:
            bad = jnp.logical_and(first_block, iidx < WIN)
            f = jnp.where(bad, 0.0, f)
        fkt[n] = f
        fb = f.astype(BF)
        fk = nt(eye, fb).astype(BF)
        fkb[n] = fk
        va = jnp.concatenate([nt(eye, vbuf[pl.ds(n * CH, CH)]), one_row], axis=0).astype(BF)
        vta[n] = va
        pre[n] = tot[...]
        tot[...] += nn(va, fk)

    each(key_chunk)
    vta[NB, :, pl.ds(0, WIN)] = jnp.concatenate(
        [nt(eye, vbuf[pl.ds(NB * CH, WIN)]), one_row[:, :WIN]], axis=0).astype(BF)
    own1[...] = split(tot[...])

    def scan_copy(o, own, got, send, recv):
        return pltpu.make_async_remote_copy(
            own, got.at[b], send.at[o], recv.at[b], device_id=ctx(place(lax.rem(b + o, NB), h)),
            device_id_type=MESH)

    def forward(o, act):
        @pl.when(b + o < NB)
        def _():
            act(scan_copy(o, own1, ag1, a1_send, a1_recv))

    def backward(o, act):
        @pl.when(b - o >= 0)
        def _():
            act(scan_copy(NB - o, own2, ag2, a2_send, a2_recv))

    for o in range(7, 0, -1):
        forward(o, go)

    arrived(2)
    scale = 1.0 / HD**0.5

    def query_chunk(n):
        q = qbuf[pl.ds(n * CH, CH)]
        f = halves(nt(w2q, q))
        fqt[n] = f
        fb = f.astype(BF)
        fqb[n] = fb
        sc = nt(kbuf[pl.ds(n * CH, CH + WIN)], q) * scale
        ci = lax.broadcasted_iota(jnp.int32, (CH + WIN, CH), 0)
        ii = lax.broadcasted_iota(jnp.int32, (CH + WIN, CH), 1)
        inwin = jnp.logical_and(ci > ii, ci <= ii + WIN)
        if n == 0:
            inwin = jnp.logical_and(inwin, jnp.logical_or(ci >= WIN, b > 0))
        sc = jnp.where(inwin, sc, -jnp.inf)
        top = jnp.max(sc, axis=0, keepdims=True)
        w = jnp.exp(sc - top).astype(BF)
        wn = nn(vta[n], w[:CH]) + nn(vta[n + 1, :, pl.ds(0, WIN)], w[CH:])
        ws = jnp.exp(jnp.minimum(top, 0.0))
        ls = jnp.exp(-jnp.maximum(top, 0.0))
        if n == 0:
            early = jnp.logical_and(first_block, lax.broadcasted_iota(jnp.int32, (1, CH), 1) < WIN)
            ws = jnp.where(early, 1.0, ws)
            ls = jnp.where(early, 0.0, ls)
        am = jnp.where(lower, nn(fkb[n], fb), 0.0).astype(BF)
        ln = nn(vta[n], am) + nn(split(pre[n]), fb)
        win[n] = ws * wn + ls * ln
        scal[n] = jnp.broadcast_to(ls, (8, CH))

    each(query_chunk)

    lin[...] = jnp.zeros((AUG, CH), F32)
    for m in range(NB - 1):
        @pl.when(m < b)
        def _():
            pltpu.make_async_copy(ag1.at[m], ag1.at[m], a1_recv.at[m]).wait()
            lin[...] += ag1[m].astype(F32)
    carry = joined(lin[...])
    carry_b = split(carry)

    def out_chunk(n):
        full = win[n] + scal[n][:1] * nn(carry_b, fqb[n])
        inv = 1.0 / full[HD : HD + 1]
        out = full[:HD] * inv
        outs[n] = out
        stu[n] = nt(eye, out.astype(BF)).astype(BF)
        scal[n] = jnp.broadcast_to(scal[n][:1] * inv, (8, CH))

    each(out_chunk)
    arrived(3)
    errors, suffix = [], [jnp.zeros((AUG, CH), F32)]

    def diff_chunk(k):
        n = NB - 1 - k
        coef, out = scal[n][:1], outs[n]
        diff = out - nt(eye, tbuf[pl.ds(n * CH, CH)])
        sq = diff * diff
        for r in range(HD // 8):
            errors.append(sq[8 * r : 8 * r + 8])
        g = diff * (2.0 / HD)
        gd = -coef * jnp.sum(g * out, axis=0, keepdims=True)
        scal[n] = jnp.broadcast_to(gd, (8, CH))
        ga = jnp.concatenate([coef * g, gd * one_row], axis=0).astype(BF)
        gna[n] = ga
        later[n] = suffix[-1]
        suffix.append(suffix[-1] + nt(ga, fqb[n]))

    each(diff_chunk)
    own2[...] = split(suffix[-1])
    while len(errors) > 1:
        errors = [sum(errors[i : i + 2]) for i in range(0, len(errors), 2)]
    la[b] = errors[0]
    for o in range(7, 0, -1):
        backward(o, go)

    def loss_a(o, act):
        act(pltpu.make_async_remote_copy(
            la.at[b], la.at[b], l_send.at[0, o], l_recv.at[0],
            device_id=ctx(place(lax.rem(b + o, NB), h)), device_id_type=MESH))

    def loss_b(o, act):
        act(pltpu.make_async_remote_copy(
            lb.at[xme], lb.at[xme], l_send.at[1, o], l_recv.at[1],
            device_id={"head": lax.rem(xme + o, 4)}, device_id_type=MESH))

    def loss_c(o, act):
        act(pltpu.make_async_remote_copy(
            lc.at[h], lc.at[h], l_send.at[2, o], l_recv.at[2],
            device_id=ctx(place(b, lax.rem(h + o, NB))), device_id_type=MESH))

    def total(ref, count, level):
        part = ref.at[pl.ds(0, count - 1)]
        pltpu.make_async_copy(part, part, l_recv.at[level]).wait()
        acc = ref[0]
        for m in range(1, count):
            acc = acc + ref[m]
        return acc

    for o in range(1, NB):
        loss_a(o, go)

    def student(j, act):
        to = NB * b + j

        def remote():
            act(pltpu.make_async_remote_copy(
                stu.at[j], stu_got.at[h], s_send.at[j], s_recv, device_id=ctx(to), device_id_type=MESH))

        pl.when(to != me)(remote)
        if act is go:
            @pl.when(to == me)
            def _():
                pltpu.make_async_copy(stu.at[j], stu_got.at[h], s_recv).start()

    for j in range(NB):
        student(j, go)

    dq = []

    def mix_chunk(n):
        gd = scal[n][:1]
        ga = gna[n]
        mx = nn(vbuf[pl.ds(n * CH, CH)], ga[:HD]) + gd
        mx = jnp.where(lower, mx, 0.0).astype(BF)
        st = nt(eye, split(pre[n] + carry)).astype(BF)
        gq = nn(fkt[n].astype(BF), mx) + nn(st, ga)
        dq.append(proj_grad(fqt[n], gq))
        lt = nt(eye, split(later[n])).astype(BF)
        gfk[n] = nt(fqb[n], mx) + nn(lt, vta[n])

    each(mix_chunk)
    grad_q = nn(jnp.concatenate(dq, axis=1), qbuf[...])
    rs_own[pl.ds(0, HF)] = grad_q.astype(BF)

    def reduce(o, act, keys):
        m = lax.rem(b + o, NB)

        @pl.when((m >= 4) if keys else (m < 4))
        def _():
            act(pltpu.make_async_remote_copy(
                rs_own.at[pl.ds(pl.multiple_of(16 * m, 16), 16)], rs_got.at[b], r_send.at[o], r_recv,
                device_id=ctx(place(m, h)), device_id_type=MESH))

    for o in range(1, NB):
        reduce(o, go, False)

    lin[...] = jnp.zeros((AUG, CH), F32)
    for m in range(1, NB):
        @pl.when(m > b)
        def _():
            pltpu.make_async_copy(ag2.at[m], ag2.at[m], a2_recv.at[m]).wait()
            lin[...] += ag2[m].astype(F32)
    after = nt(eye, split(joined(lin[...]))).astype(BF)
    dk = []

    def key_grad(n):
        dk.append(proj_grad(fkt[n], gfk[n] + nn(after, vta[n])))

    each(key_grad)
    grad_k = nn(jnp.concatenate(dk, axis=1), kbuf[pl.ds(0, NB * CH)])
    rs_own[pl.ds(HF, HF)] = grad_k.astype(BF)

    for o in range(1, NB):
        reduce(o, go, True)
    rs_got[b] = rs_own[pl.ds(pl.multiple_of(16 * b, 16), 16)]
    lb[xme] = total(la, NB, 0)
    for o in range(1, 4):
        loss_b(o, go)
    part = rs_got.at[pl.ds(0, NB - 1)]
    pltpu.make_async_copy(part, part, r_recv).wait()
    acc = rs_got[0].astype(F32)
    for m in range(1, NB):
        acc = acc + rs_got[m].astype(F32)
    fin[...] = acc.astype(BF)
    slot = NB * h + b

    for o in FAR:
        for p in (2, 1, 3, 0):
            for d in range(2):
                if o or p or d:
                    pltpu.make_async_remote_copy(
                        fin, fin_out.at[slot], f_send, f_recv,
                        device_id=ctx(16 * lax.rem(y + p, 4) + 2 * lax.rem(z + o, NB) + lax.rem(c + d, 2)),
                        device_id_type=MESH).start()
    pltpu.make_async_copy(fin, fin_out.at[slot], f_recv).start()

    lc[h] = total(lb, 4, 1)
    for o in range(1, NB):
        loss_c(o, go)
    pltpu.make_async_copy(stu_got, stu_got, s_recv).wait()
    stu_t[...] = jnp.swapaxes(stu_got[...], 0, 1)
    put = pltpu.make_async_copy(stu_t, stu_out, out_sem)
    put.start()

    for o in range(NB):
        for a in range(4):
            exchange(a, o, sent)

    @pl.when(tail)
    def _():
        for o in range(NB):
            halo(0, o, sent)
            halo(1, o, sent)

    for o in range(1, NB):
        forward(o, sent)
        backward(o, sent)
        loss_a(o, sent)
        loss_c(o, sent)
        reduce(o, sent, False)
        reduce(o, sent, True)
    for o in range(1, 4):
        loss_b(o, sent)
    for j in range(NB):
        student(j, sent)
    loss_out[0, 0] = jnp.sum(total(lc, NB, 2)) * (1.0 / (8192 * 32 * 128))
    put.wait()
    part = fin_out.at[pl.ds(0, 63)]
    pltpu.make_async_copy(part, part, f_send).wait()
    pltpu.make_async_copy(fin_out, fin_out, f_recv).wait()


def per_device(queries, keys, values, teacher, wq, wk):
    hbm = pl.BlockSpec(memory_space=pl.ANY)
    dma = pltpu.SemaphoreType.DMA
    stu, fin, loss = pl.pallas_call(
        kernel,
        out_shape=(
            jax.ShapeDtypeStruct((CH, NB, HD), BF),
            jax.ShapeDtypeStruct((NB * NB, 16, HD), BF),
            jax.ShapeDtypeStruct((1, 1), F32),
        ),
        in_specs=[hbm] * 6,
        out_specs=(hbm, hbm, pl.BlockSpec(memory_space=pltpu.SMEM)),
        scratch_shapes=[
            pltpu.VMEM((4, CH, NB, HD), BF),
            pltpu.VMEM((4, NB, CH, HD), BF),
            pltpu.VMEM((NB, HF, HD), BF),
            pltpu.VMEM((NB, HF, HD), BF),
            pltpu.VMEM((NB * CH + WIN, HD), BF),
            pltpu.VMEM((NB * CH + WIN, HD), BF),
            pltpu.VMEM((NB * CH, HD), BF),
            pltpu.VMEM((NB * CH, HD), BF),
            pltpu.VMEM((NB, CH, CH), F32),
            pltpu.VMEM((NB, CH, CH), BF),
            pltpu.VMEM((NB, CH, CH), F32),
            pltpu.VMEM((NB, CH, CH), BF),
            pltpu.VMEM((NB + 1, AUG, CH), BF),
            pltpu.VMEM((NB, AUG, CH), F32),
            pltpu.VMEM((AUG, CH), F32),
            pltpu.VMEM((NB, AUG, CH), F32),
            pltpu.VMEM((NB, HD, CH), F32),
            pltpu.VMEM((AUG, CH), F32),
            pltpu.VMEM((NB, AUG, CH), BF),
            pltpu.VMEM((NB, CH, CH), F32),
            pltpu.VMEM((NB, AUG, CH), F32),
            pltpu.VMEM((AUG, CH), BF),
            pltpu.VMEM((NB, AUG, CH), BF),
            pltpu.VMEM((AUG, CH), BF),
            pltpu.VMEM((NB, AUG, CH), BF),
            pltpu.VMEM((NB, CH, HD), BF),
            pltpu.VMEM((NB, CH, HD), BF),
            pltpu.VMEM((CH, NB, HD), BF),
            pltpu.VMEM((2 * HF, HD), BF),
            pltpu.VMEM((NB, 16, HD), BF),
            pltpu.VMEM((16, HD), BF),
            pltpu.VMEM((NB, 8, CH), F32),
            pltpu.VMEM((4, 8, CH), F32),
            pltpu.VMEM((NB, 8, CH), F32),
            pltpu.VMEM((NB, 8, CH), F32),
            dma((4,)), dma((2,)), dma,
            dma((4, NB)), dma((4,)),
            dma((2, NB)), dma((2,)),
            dma((NB,)), dma((NB,)),
            dma((NB,)), dma((NB,)),
            dma((NB,)), dma,
            dma((NB,)), dma,
            dma, dma,
            dma((3, NB)), dma((3,)),
        ],
        compiler_params=pltpu.CompilerParams(collective_id=0, has_side_effects=True),
    )(queries, keys, values, teacher, wq, wk)
    grads = fin.reshape(NB, 2 * HF, HD)
    return stu, loss[0, 0], grads[:, :HF].astype(F32), grads[:, HF:].astype(F32)


def solution(mesh):
    tok = P("ctx", "head", None)
    par = P("head", None, None)
    return jax.shard_map(
        per_device,
        mesh=mesh,
        in_specs=(tok, tok, tok, tok, par, par),
        out_specs=(tok, P(), par, par),
        check_vma=False,
    )
```

```python
import jax
import jax.numpy as jnp
from jax import lax
from jax.experimental import pallas as pl
from jax.experimental.pallas import tpu as pltpu
from jax.sharding import PartitionSpec as P

NB = 8
CH = 128
WIN = 64
HD = 128
HF = 64
AUG = 144
FAR = (4, 3, 5, 2, 6, 1, 7, 0)
MESH = pl.DeviceIdType.MESH
BF = jnp.bfloat16
F32 = jnp.float32


def nt(a, b):
    return lax.dot_general(a, b, (((1,), (1,)), ((), ())), preferred_element_type=F32)


def nn(a, b):
    return jnp.dot(a, b, preferred_element_type=F32)


def halves(proj):
    e = []
    for s in (proj[:HF], proj[HF:]):
        w = jnp.exp(s - jnp.max(s, axis=0, keepdims=True))
        e.append(w * (1.0 / jnp.sum(w, axis=0, keepdims=True)))
    return jnp.concatenate(e, axis=0)


def proj_grad(feat, grad):
    d = []
    for a in (0, HF):
        u, g = feat[a : a + HF], grad[a : a + HF]
        d.append(u * (g - jnp.sum(u * g, axis=0, keepdims=True)))
    return (d[0] - d[1]).astype(BF)


def split(x):
    norm = x[HD : HD + 1]
    high = norm.astype(BF).astype(F32)
    row = lax.broadcasted_iota(jnp.int32, (AUG - HD, CH), 0)
    aug = jnp.where(row == 0, high, jnp.where(row == 1, norm - high, 0.0))
    return jnp.concatenate([x[:HD], aug], axis=0).astype(BF)


def joined(x):
    return jnp.concatenate([x[:HD], x[HD : HD + 8] + pltpu.roll(x[HD : HD + 8], 7, 0), x[HD + 8 :]], axis=0)


def place(block, head):
    return 16 * (block // 2) + 2 * head + lax.rem(block, 2)


def each(body):
    for n in range(NB):
        body(n)


def kernel(
    q_hbm, k_hbm, v_hbm, t_hbm, wq_hbm, wk_hbm,
    stu_out, fin_out, loss_out,
    xin, xs, wq_ref, wk_ref,
    kbuf, vbuf, qbuf, tbuf, fkt, fkb, fqt, fqb, vta, pre, win, outs, lin, gna, gfk, later,
    own1, ag1, own2, ag2, stu, stu_got, stu_t, gsum, fin, la, lb, lc, loss, scal,
    in_sem, w_sem, out_sem, loss_sem,
    x_send, x_recv, h_send, h_recv, a1_send, a1_recv, a2_send, a2_recv,
    s_send, s_recv, r_send, r_recv, f_send, f_recv, l_send, l_recv,
):
    me = lax.axis_index("ctx")
    xme = lax.axis_index("head")
    src_b, src_j = me // NB, lax.rem(me, NB)
    b = 2 * (me // 16) + lax.rem(me, 2)
    h = lax.rem(me, 16) // 2
    first_block = b == 0

    def ctx(i):
        return {"ctx": i}

    y, z, c = me // 16, h, lax.rem(me, 2)
    k_in, v_in, q_in, t_in = (xs.at[a] for a in range(4))
    loads = [pltpu.make_async_copy(src, xin.at[a], in_sem.at[a]) for a, src in enumerate((k_hbm, v_hbm, q_hbm, t_hbm))]
    weights = [
        pltpu.make_async_copy(wq_hbm, wq_ref, w_sem.at[0]),
        pltpu.make_async_copy(wk_hbm, wk_ref, w_sem.at[1]),
    ]

    bar = pltpu.get_barrier_semaphore()

    def greet(device):
        pl.semaphore_signal(bar, inc=1, device_id=device, device_id_type=MESH)

    for o in FAR:
        for d in range(2):
            if o or d:
                greet(ctx(16 * y + 2 * lax.rem(z + o, NB) + lax.rem(c + d, 2)))
    for o in range(1, 4):
        for d in range(2):
            greet(ctx(16 * lax.rem(y + o, 4) + 2 * z + d))
        greet({"head": lax.rem(xme + o, 4)})
    gives = jnp.logical_and(lax.rem(me, 16) == 15, y < 3)
    takes = jnp.logical_and(c == 0, y > 0)

    @pl.when(gives)
    def _():
        for o in range(NB):
            greet(ctx(16 * (y + 1) + 2 * o))

    @pl.when(takes)
    def _():
        greet(ctx(16 * (y - 1) + 15))

    for load in loads + weights:
        load.start()
    for a in range(4):
        loads[a].wait()
        xs[a] = jnp.swapaxes(xin[a], 0, 1)
    for load in weights:
        load.wait()
    pl.semaphore_wait(bar, 24 + 8 * gives.astype(jnp.int32) + takes.astype(jnp.int32))

    arrays = ((k_in, kbuf, WIN), (v_in, vbuf, WIN), (q_in, qbuf, 0), (t_in, tbuf, 0))

    def exchange(a, o, act):
        src, dst, base = arrays[a]
        hd = lax.rem(h + o, NB)
        to = place(src_b, hd)
        rows = dst.at[pl.ds(pl.multiple_of(base + CH * src_j, WIN), CH)]

        def remote():
            act(pltpu.make_async_remote_copy(
                src.at[hd], rows, x_send.at[a], x_recv.at[a], device_id=ctx(to), device_id_type=MESH))

        if o == 0:
            pl.when(to != me)(remote)
            if act is go:
                @pl.when(to == me)
                def _():
                    pltpu.make_async_copy(src.at[hd], rows, x_recv.at[a]).start()
        else:
            remote()

    def go(c):
        c.start()

    def sent(c):
        c.wait_send()

    tail = jnp.logical_and(src_j == NB - 1, src_b < NB - 1)

    def halo(a, o, act):
        src, dst, _ = arrays[a]
        hd = lax.rem(h + o, NB)
        to = place(src_b + 1, hd)

        def remote():
            act(pltpu.make_async_remote_copy(
                src.at[hd, pl.ds(CH - WIN, WIN)], dst.at[pl.ds(0, WIN)], h_send.at[a], h_recv.at[a],
                device_id=ctx(to), device_id_type=MESH))

        if o == 0:
            pl.when(to != me)(remote)
            if act is go:
                @pl.when(to == me)
                def _():
                    pltpu.make_async_copy(
                        src.at[hd, pl.ds(CH - WIN, WIN)], dst.at[pl.ds(0, WIN)], h_recv.at[a]).start()
        else:
            remote()

    for a in range(4):
        for o in FAR:
            exchange(a, o, go)
        if a < 2:
            @pl.when(tail)
            def _():
                for o in FAR:
                    halo(a, o, go)

    @pl.when(first_block)
    def _():
        kbuf[pl.ds(0, WIN)] = jnp.zeros((WIN, HD), BF)
        vbuf[pl.ds(0, WIN)] = jnp.zeros((WIN, HD), BF)

    eye = jnp.where(
        lax.broadcasted_iota(jnp.int32, (CH, CH), 0) == lax.broadcasted_iota(jnp.int32, (CH, CH), 1),
        1.0, 0.0).astype(BF)
    one_row = jnp.where(lax.broadcasted_iota(jnp.int32, (AUG - HD, CH), 0) < 2, 1.0, 0.0)
    wq1, wk1 = wq_ref[h], wk_ref[h]
    w2q = jnp.concatenate([wq1, -wq1], axis=0)
    w2k = jnp.concatenate([wk1, -wk1], axis=0)

    def arrived(a):
        src, dst, base = arrays[a]
        part = dst.at[pl.ds(base, NB * CH)]
        pltpu.make_async_copy(part, part, x_recv.at[a]).wait()

    def halo_arrived(a):
        dst = arrays[a][1]
        part = dst.at[pl.ds(0, WIN)]
        pltpu.make_async_copy(part, part, h_recv.at[a]).wait()

    arrived(0)

    @pl.when(b > 0)
    def _():
        halo_arrived(0)

    cidx = lax.broadcasted_iota(jnp.int32, (CH, CH), 0)
    iidx = lax.broadcasted_iota(jnp.int32, (CH, CH), 1)
    lower = cidx <= iidx

    sums = [jnp.zeros((AUG, CH), F32)]

    def key_chunk(n):
        f = halves(nt(w2k, kbuf[pl.ds(n * CH, CH)]))
        if n == 0:
            bad = jnp.logical_and(first_block, iidx < WIN)
            f = jnp.where(bad, 0.0, f)
        fkt[n] = f
        fb = f.astype(BF)
        fk = nt(eye, fb).astype(BF)
        fkb[n] = fk

    each(key_chunk)
    arrived(1)

    @pl.when(b > 0)
    def _():
        halo_arrived(1)

    def value_chunk(n):
        va = jnp.concatenate([nt(eye, vbuf[pl.ds(n * CH, CH)]), one_row], axis=0).astype(BF)
        vta[n] = va
        pre[n] = sums[-1]
        sums.append(sums[-1] + nn(va, fkb[n]))

    each(value_chunk)
    vta[NB, :, pl.ds(0, WIN)] = jnp.concatenate(
        [nt(eye, vbuf[pl.ds(NB * CH, WIN)]), one_row[:, :WIN]], axis=0).astype(BF)
    own1[...] = split(sums[-1])

    def scan_copy(o, own, got, send, recv):
        return pltpu.make_async_remote_copy(
            own, got.at[b], send.at[o], recv.at[b], device_id=ctx(place(lax.rem(b + o, NB), h)),
            device_id_type=MESH)

    def forward(o, act):
        @pl.when(b + o < NB)
        def _():
            act(scan_copy(o, own1, ag1, a1_send, a1_recv))

    def backward(o, act):
        @pl.when(b - o >= 0)
        def _():
            act(scan_copy(NB - o, own2, ag2, a2_send, a2_recv))

    for o in range(7, 0, -1):
        forward(o, go)

    arrived(2)
    scale = 1.0 / HD**0.5

    def query_chunk(n):
        q = qbuf[pl.ds(n * CH, CH)]
        f = halves(nt(w2q, q))
        fqt[n] = f
        fb = f.astype(BF)
        fqb[n] = fb
        sc = nt(kbuf[pl.ds(n * CH, CH + WIN)], q) * scale
        ci = lax.broadcasted_iota(jnp.int32, (CH + WIN, CH), 0)
        ii = lax.broadcasted_iota(jnp.int32, (CH + WIN, CH), 1)
        inwin = jnp.logical_and(ci > ii, ci <= ii + WIN)
        if n == 0:
            inwin = jnp.logical_and(inwin, jnp.logical_or(ci >= WIN, b > 0))
        sc = jnp.where(inwin, sc, -jnp.inf)
        top = jnp.max(sc, axis=0, keepdims=True)
        w = jnp.exp(sc - top).astype(BF)
        wn = nn(vta[n], w[:CH]) + nn(vta[n + 1, :, pl.ds(0, WIN)], w[CH:])
        ws = jnp.exp(jnp.minimum(top, 0.0))
        ls = jnp.exp(-jnp.maximum(top, 0.0))
        if n == 0:
            early = jnp.logical_and(first_block, lax.broadcasted_iota(jnp.int32, (1, CH), 1) < WIN)
            ws = jnp.where(early, 1.0, ws)
            ls = jnp.where(early, 0.0, ls)
        am = jnp.where(lower, nn(fkb[n], fb), 0.0).astype(BF)
        ln = nn(vta[n], am) + nn(split(pre[n]), fb)
        win[n] = ws * wn + ls * ln
        scal[n] = jnp.broadcast_to(ls, (8, CH))

    each(query_chunk)

    lin[...] = jnp.zeros((AUG, CH), F32)
    for m in range(NB - 1):
        @pl.when(m < b)
        def _():
            pltpu.make_async_copy(ag1.at[m], ag1.at[m], a1_recv.at[m]).wait()
            lin[...] += ag1[m].astype(F32)
    carry = joined(lin[...])
    carry_b = split(carry)

    def out_chunk(n):
        full = win[n] + scal[n][:1] * nn(carry_b, fqb[n])
        inv = 1.0 / full[HD : HD + 1]
        out = full[:HD] * inv
        outs[n] = out
        scal[n] = jnp.broadcast_to(scal[n][:1] * inv, (8, CH))

    each(out_chunk)
    arrived(3)
    errors, suffix = [], [jnp.zeros((AUG, CH), F32)]

    def diff_chunk(k):
        n = NB - 1 - k
        coef, out = scal[n][:1], outs[n]
        diff = out - nt(eye, tbuf[pl.ds(n * CH, CH)])
        sq = diff * diff
        for r in range(HD // 8):
            errors.append(sq[8 * r : 8 * r + 8])
        g = diff * (2.0 / HD)
        gd = -coef * jnp.sum(g * out, axis=0, keepdims=True)
        scal[n] = jnp.broadcast_to(gd, (8, CH))
        ga = jnp.concatenate([coef * g, gd * one_row], axis=0).astype(BF)
        gna[n] = ga
        later[n] = suffix[-1]
        suffix.append(suffix[-1] + nt(ga, fqb[n]))

    each(diff_chunk)
    own2[...] = split(suffix[-1])
    while len(errors) > 1:
        errors = [sum(errors[i : i + 2]) for i in range(0, len(errors), 2)]
    la[b] = errors[0]
    for o in range(7, 0, -1):
        backward(o, go)

    def loss_a(o, act):
        act(pltpu.make_async_remote_copy(
            la.at[b], la.at[b], l_send.at[0], l_recv.at[0],
            device_id=ctx(place(lax.rem(b + o, NB), h)), device_id_type=MESH))

    def loss_b(o, act):
        act(pltpu.make_async_remote_copy(
            lb.at[xme], lb.at[xme], l_send.at[1], l_recv.at[1],
            device_id={"head": lax.rem(xme + o, 4)}, device_id_type=MESH))

    def loss_c(o, act):
        act(pltpu.make_async_remote_copy(
            lc.at[h], lc.at[h], l_send.at[2], l_recv.at[2],
            device_id=ctx(place(b, lax.rem(h + o, NB))), device_id_type=MESH))

    def total(ref, count, level):
        part = ref.at[pl.ds(0, count - 1)]
        pltpu.make_async_copy(part, part, l_recv.at[level]).wait()
        acc = ref[0]
        for m in range(1, count):
            acc = acc + ref[m]
        return acc

    for o in range(1, NB):
        loss_a(o, go)

    def student(j, act):
        to = NB * b + j

        def remote():
            act(pltpu.make_async_remote_copy(
                stu.at[j], stu_got.at[h], s_send, s_recv, device_id=ctx(to), device_id_type=MESH))

        pl.when(to != me)(remote)
        if act is go:
            @pl.when(to == me)
            def _():
                pltpu.make_async_copy(stu.at[j], stu_got.at[h], s_recv).start()

    for j in range(NB):
        stu[j] = nt(eye, outs[j].astype(BF)).astype(BF)
    for j in range(NB):
        student(j, go)

    dq = []

    def mix_chunk(n):
        gd = scal[n][:1]
        ga = gna[n]
        mx = nn(vbuf[pl.ds(n * CH, CH)], ga[:HD]) + gd
        mx = jnp.where(lower, mx, 0.0).astype(BF)
        st = nt(eye, split(pre[n] + carry)).astype(BF)
        gq = nn(fkt[n].astype(BF), mx) + nn(st, ga)
        dq.append(proj_grad(fqt[n], gq))
        lt = nt(eye, split(later[n])).astype(BF)
        gfk[n] = nt(fqb[n], mx) + nn(lt, vta[n])

    each(mix_chunk)
    gsum[0, b] = nn(jnp.concatenate(dq, axis=1), qbuf[...]).astype(BF)

    def share(w, o, act):
        act(pltpu.make_async_remote_copy(
            gsum.at[w, b], gsum.at[w, b], r_send.at[w], r_recv.at[w],
            device_id=ctx(place(lax.rem(b + o, NB), h)), device_id_type=MESH))

    def summed(w):
        part = gsum.at[w, pl.ds(0, NB - 1)]
        pltpu.make_async_copy(part, part, r_recv.at[w]).wait()
        acc = gsum[w, 0].astype(F32)
        for m in range(1, NB):
            acc = acc + gsum[w, m].astype(F32)
        fin[w] = acc.astype(BF)

    def spread(w, o, act):
        act(pltpu.make_async_remote_copy(
            fin.at[w], fin_out.at[w, h], f_send.at[w], f_recv.at[w],
            device_id=ctx(place(b, lax.rem(h + o, NB))), device_id_type=MESH))

    def spread_all(w):
        for o in FAR[:-1]:
            spread(w, o, go)
        pltpu.make_async_copy(fin.at[w], fin_out.at[w, h], f_recv.at[w]).start()

    for o in range(1, NB):
        share(0, o, go)
    lb[xme] = total(la, NB, 0)
    for o in range(1, 4):
        loss_b(o, go)

    lin[...] = jnp.zeros((AUG, CH), F32)
    for m in range(1, NB):
        @pl.when(m > b)
        def _():
            pltpu.make_async_copy(ag2.at[m], ag2.at[m], a2_recv.at[m]).wait()
            lin[...] += ag2[m].astype(F32)
    after = nt(eye, split(joined(lin[...]))).astype(BF)
    dk = []

    def key_grad(n):
        dk.append(proj_grad(fkt[n], gfk[n] + nn(after, vta[n])))

    each(key_grad)
    gsum[1, b] = nn(jnp.concatenate(dk, axis=1), kbuf[pl.ds(0, NB * CH)]).astype(BF)
    for o in range(1, NB):
        share(1, o, go)
    summed(0)
    spread_all(0)
    summed(1)
    spread_all(1)

    lc[h] = total(lb, 4, 1)
    for o in range(1, NB):
        loss_c(o, go)
    pltpu.make_async_copy(stu_got, stu_got, s_recv).wait()
    stu_t[...] = jnp.swapaxes(stu_got[...], 0, 1)
    put = pltpu.make_async_copy(stu_t, stu_out, out_sem)
    put.start()

    def left(ref, sem):
        pltpu.make_async_copy(ref, ref, sem).wait()

    own = (me == place(src_b, h)).astype(jnp.int32)
    for n in range(2):
        @pl.when(own == n)
        def _():
            for a in range(4):
                left(qbuf.at[pl.ds(0, CH * (NB - n))], x_send.at[a])
            left(stu.at[pl.ds(0, NB - n)], s_send)

        @pl.when(jnp.logical_and(tail, (me == place(src_b + 1, h)).astype(jnp.int32) == n))
        def _():
            for a in range(2):
                left(qbuf.at[pl.ds(0, WIN * (NB - n))], h_send.at[a])

    for o in range(1, NB):
        forward(o, sent)
        backward(o, sent)
    left(la.at[pl.ds(0, NB - 1)], l_send.at[0])
    left(lb.at[pl.ds(0, 3)], l_send.at[1])
    left(lc.at[pl.ds(0, NB - 1)], l_send.at[2])
    for w in range(2):
        left(gsum.at[w, pl.ds(0, NB - 1)], r_send.at[w])
        left(gsum.at[w, pl.ds(0, NB - 1)], f_send.at[w])
    loss[...] = jnp.sum(total(lc, NB, 2), keepdims=True) * (1.0 / (8192 * 32 * 128))
    put_loss = pltpu.make_async_copy(loss, loss_out, loss_sem)
    put_loss.start()
    put.wait()
    put_loss.wait()
    for w in range(2):
        pltpu.make_async_copy(fin_out.at[w], fin_out.at[w], f_recv.at[w]).wait()


def finish(stu_in, fin_in, loss_in, stu_out, gq_out, gk_out, loss_out, fin, gq, gk, loss, in_sem, out_sem):
    loads = [
        pltpu.make_async_copy(src, dst, in_sem.at[i])
        for i, (src, dst) in enumerate(((fin_in, fin), (loss_in, loss)))
    ]
    stores = [
        pltpu.make_async_copy(src, dst, out_sem.at[i])
        for i, (src, dst) in enumerate(((gq, gq_out), (gk, gk_out), (loss, loss_out), (stu_in, stu_out)))
    ]
    for load in loads:
        load.start()
    stores[3].start()
    loads[0].wait()
    gq[...] = fin[0].astype(F32)
    stores[0].start()
    gk[...] = fin[1].astype(F32)
    stores[1].start()
    loads[1].wait()
    stores[2].start()
    for store in stores:
        store.wait()


def per_device(queries, keys, values, teacher, wq, wk):
    anywhere = pl.BlockSpec(memory_space=pl.ANY)
    dma = pltpu.SemaphoreType.DMA
    stu, fin, loss = pl.pallas_call(
        kernel,
        out_shape=(
            jax.ShapeDtypeStruct((CH, NB, HD), BF),
            jax.ShapeDtypeStruct((2, NB, HF, HD), BF),
            jax.ShapeDtypeStruct((1, 1), F32),
        ),
        in_specs=[anywhere] * 6,
        out_specs=(anywhere,) * 3,
        scratch_shapes=[
            pltpu.VMEM((4, CH, NB, HD), BF),
            pltpu.VMEM((4, NB, CH, HD), BF),
            pltpu.VMEM((NB, HF, HD), BF),
            pltpu.VMEM((NB, HF, HD), BF),
            pltpu.VMEM((NB * CH + WIN, HD), BF),
            pltpu.VMEM((NB * CH + WIN, HD), BF),
            pltpu.VMEM((NB * CH, HD), BF),
            pltpu.VMEM((NB * CH, HD), BF),
            pltpu.VMEM((NB, CH, CH), F32),
            pltpu.VMEM((NB, CH, CH), BF),
            pltpu.VMEM((NB, CH, CH), F32),
            pltpu.VMEM((NB, CH, CH), BF),
            pltpu.VMEM((NB + 1, AUG, CH), BF),
            pltpu.VMEM((NB, AUG, CH), F32),
            pltpu.VMEM((NB, AUG, CH), F32),
            pltpu.VMEM((NB, HD, CH), F32),
            pltpu.VMEM((AUG, CH), F32),
            pltpu.VMEM((NB, AUG, CH), BF),
            pltpu.VMEM((NB, CH, CH), F32),
            pltpu.VMEM((NB, AUG, CH), F32),
            pltpu.VMEM((AUG, CH), BF),
            pltpu.VMEM((NB, AUG, CH), BF),
            pltpu.VMEM((AUG, CH), BF),
            pltpu.VMEM((NB, AUG, CH), BF),
            pltpu.VMEM((NB, CH, HD), BF),
            pltpu.VMEM((NB, CH, HD), BF),
            pltpu.VMEM((CH, NB, HD), BF),
            pltpu.VMEM((2, NB, HF, HD), BF),
            pltpu.VMEM((2, HF, HD), BF),
            pltpu.VMEM((NB, 8, CH), F32),
            pltpu.VMEM((4, 8, CH), F32),
            pltpu.VMEM((NB, 8, CH), F32),
            pltpu.VMEM((1, 1), F32),
            pltpu.VMEM((NB, 8, CH), F32),
            dma((4,)), dma((2,)), dma, dma,
            dma((4,)), dma((4,)),
            dma((2,)), dma((2,)),
            dma((NB,)), dma((NB,)),
            dma((NB,)), dma((NB,)),
            dma, dma,
            dma((2,)), dma((2,)),
            dma((2,)), dma((2,)),
            dma((3,)), dma((3,)),
        ],
        compiler_params=pltpu.CompilerParams(
            collective_id=0, has_side_effects=True, vmem_limit_bytes=24 * 2**20),
    )(*(pltpu.with_memory_space_constraint(x, pltpu.HBM) for x in (queries, keys, values, teacher, wq, wk)))
    stu, gq, gk, loss = pl.pallas_call(
        finish,
        out_shape=(
            jax.ShapeDtypeStruct((CH, NB, HD), BF),
            jax.ShapeDtypeStruct((NB, HF, HD), F32),
            jax.ShapeDtypeStruct((NB, HF, HD), F32),
            jax.ShapeDtypeStruct((1, 1), F32),
        ),
        in_specs=[anywhere] * 3,
        out_specs=(anywhere,) * 4,
        scratch_shapes=[
            pltpu.VMEM((2, NB, HF, HD), BF),
            pltpu.VMEM((NB, HF, HD), F32),
            pltpu.VMEM((NB, HF, HD), F32),
            pltpu.VMEM((1, 1), F32),
            dma((2,)),
            dma((4,)),
        ],
        compiler_params=pltpu.CompilerParams(vmem_limit_bytes=8 * 2**20),
    )(stu, fin, loss)
    return stu, loss[0, 0], gq, gk


def solution(mesh):
    tok = P("ctx", "head", None)
    par = P("head", None, None)
    return jax.shard_map(
        per_device,
        mesh=mesh,
        in_specs=(tok, tok, tok, tok, par, par),
        out_specs=(tok, P(), par, par),
        check_vma=False,
    )
```

```python
import jax
import jax.numpy as jnp
from jax import lax
from jax.experimental import pallas as pl
from jax.experimental.pallas import tpu as pltpu
from jax.sharding import PartitionSpec as P

NB = 8
CH = 128
WIN = 64
HD = 128
HF = 64
AUG = 144
FAR = (4, 3, 5, 2, 6, 1, 7, 0)
MESH = pl.DeviceIdType.MESH
BF = jnp.bfloat16
F32 = jnp.float32


def nt(a, b):
    return lax.dot_general(a, b, (((1,), (1,)), ((), ())), preferred_element_type=F32)


def nn(a, b):
    return jnp.dot(a, b, preferred_element_type=F32)


def halves(proj):
    e = []
    for s in (proj[:HF], proj[HF:]):
        w = jnp.exp(s - jnp.max(s, axis=0, keepdims=True))
        e.append(w * (1.0 / jnp.sum(w, axis=0, keepdims=True)))
    return jnp.concatenate(e, axis=0)


def proj_grad(feat, grad):
    d = []
    for a in (0, HF):
        u, g = feat[a : a + HF], grad[a : a + HF]
        d.append(u * (g - jnp.sum(u * g, axis=0, keepdims=True)))
    return (d[0] - d[1]).astype(BF)


def split(x):
    norm = x[HD : HD + 1]
    high = norm.astype(BF).astype(F32)
    row = lax.broadcasted_iota(jnp.int32, (AUG - HD, CH), 0)
    aug = jnp.where(row == 0, high, jnp.where(row == 1, norm - high, 0.0))
    return jnp.concatenate([x[:HD], aug], axis=0).astype(BF)


def joined(x):
    return jnp.concatenate([x[:HD], x[HD : HD + 8] + pltpu.roll(x[HD : HD + 8], 7, 0), x[HD + 8 :]], axis=0)


def place(block, head):
    return 16 * (block // 2) + 2 * head + lax.rem(block, 2)


def each(body):
    for n in range(NB):
        body(n)


def kernel(
    q_hbm, k_hbm, v_hbm, t_hbm, wq_hbm, wk_hbm,
    stu_out, fin_out, loss_out,
    xin, xs, wq_ref, wk_ref,
    kbuf, vbuf, qbuf, tbuf, fkt, fkb, fqt, fqb, vta, pre, win, outs, lin, gna, gfk, later,
    own1, ag1, own2, ag2, stu, stu_got, stu_t, gpart, gsum, fin, la, lb, lc, loss, scal, mask,
    in_sem, w_sem, out_sem, loss_sem,
    x_send, x_recv, h_send, h_recv, a_send, a1_recv, a2_recv,
    s_send, s_recv, r_send, r_recv, f_send, f_recv, g_send, g_recv, l_send, l_recv,
):
    me = lax.axis_index("ctx")
    xme = lax.axis_index("head")
    src_b, src_j = me // NB, lax.rem(me, NB)
    b = 2 * (me // 16) + lax.rem(me, 2)
    h = lax.rem(me, 16) // 2
    first_block = b == 0

    def ctx(i):
        return {"ctx": i}

    y, z, c = me // 16, h, lax.rem(me, 2)
    k_in, v_in, q_in, t_in = (xs.at[a] for a in range(4))
    loads = [pltpu.make_async_copy(src, xin.at[a], in_sem.at[a]) for a, src in enumerate((k_hbm, v_hbm, q_hbm, t_hbm))]
    weights = [
        pltpu.make_async_copy(wq_hbm, wq_ref, w_sem.at[0]),
        pltpu.make_async_copy(wk_hbm, wk_ref, w_sem.at[1]),
    ]

    bar = pltpu.get_barrier_semaphore()

    def greet(device):
        pl.semaphore_signal(bar, inc=1, device_id=device, device_id_type=MESH)

    for o in FAR:
        for d in range(2):
            if o or d:
                greet(ctx(16 * y + 2 * lax.rem(z + o, NB) + lax.rem(c + d, 2)))
    for o in range(1, 4):
        for d in range(2):
            greet(ctx(16 * lax.rem(y + o, 4) + 2 * z + d))
        greet({"head": lax.rem(xme + o, 4)})
    for load in loads + weights:
        load.start()
    for a in range(4):
        loads[a].wait()
        xs[a] = jnp.swapaxes(xin[a], 0, 1)
    for load in weights:
        load.wait()
    pl.semaphore_wait(bar, 24)

    arrays = ((k_in, kbuf, WIN), (v_in, vbuf, WIN), (q_in, qbuf, 0), (t_in, tbuf, 0))

    def exchange(a, o, act):
        src, dst, base = arrays[a]
        hd = lax.rem(h + o, NB)
        to = place(src_b, hd)
        rows = dst.at[pl.ds(pl.multiple_of(base + CH * src_j, WIN), CH)]

        def remote():
            act(pltpu.make_async_remote_copy(
                src.at[hd], rows, x_send, x_recv.at[a], device_id=ctx(to), device_id_type=MESH))

        if o == 0:
            pl.when(to != me)(remote)
            if act is go:
                @pl.when(to == me)
                def _():
                    pltpu.make_async_copy(src.at[hd], rows, x_recv.at[a]).start()
        else:
            remote()

    def left(ref, sem):
        pltpu.make_async_copy(ref, ref, sem).wait()

    def go(c):
        c.start()

    def sent(c):
        c.wait_send()

    def halo(a, act):
        dst = arrays[a][1]

        @pl.when(b < NB - 1)
        def _():
            act(pltpu.make_async_remote_copy(
                dst.at[pl.ds(NB * CH, WIN)], dst.at[pl.ds(0, WIN)], h_send.at[a], h_recv.at[a],
                device_id=ctx(place(b + 1, h)), device_id_type=MESH))

    for a in range(4):
        for o in FAR:
            exchange(a, o, go)

    @pl.when(first_block)
    def _():
        kbuf[pl.ds(0, WIN)] = jnp.zeros((WIN, HD), BF)
        vbuf[pl.ds(0, WIN)] = jnp.zeros((WIN, HD), BF)

    ci = lax.broadcasted_iota(jnp.int32, (CH + WIN, CH), 0)
    ii = lax.broadcasted_iota(jnp.int32, (CH + WIN, CH), 1)
    inwin = jnp.logical_and(ci > ii, ci <= ii + WIN)
    mask[0] = jnp.where(jnp.logical_and(inwin, jnp.logical_or(ci >= WIN, b > 0)), 0.0, -jnp.inf)
    mask[1] = jnp.where(inwin, 0.0, -jnp.inf)
    eye = jnp.where(
        lax.broadcasted_iota(jnp.int32, (CH, CH), 0) == lax.broadcasted_iota(jnp.int32, (CH, CH), 1),
        1.0, 0.0).astype(BF)
    one_row = jnp.where(lax.broadcasted_iota(jnp.int32, (AUG - HD, CH), 0) < 2, 1.0, 0.0)
    wq1, wk1 = wq_ref[h], wk_ref[h]
    w2q = jnp.concatenate([wq1, -wq1], axis=0)
    w2k = jnp.concatenate([wk1, -wk1], axis=0)

    def arrived(a):
        src, dst, base = arrays[a]
        part = dst.at[pl.ds(base, NB * CH)]
        pltpu.make_async_copy(part, part, x_recv.at[a]).wait()

    arrived(0)
    halo(0, go)

    cidx = lax.broadcasted_iota(jnp.int32, (CH, CH), 0)
    iidx = lax.broadcasted_iota(jnp.int32, (CH, CH), 1)
    lower = cidx <= iidx

    def edges(buf):
        return jnp.concatenate([buf[pl.ds(WIN, WIN)], buf[pl.ds(NB * CH, WIN)]], axis=0)

    def key_chunk(n):
        f = halves(nt(w2k, kbuf[pl.ds(n * CH, CH)]))
        if n == 0:
            bad = jnp.logical_and(first_block, iidx < WIN)
            f = jnp.where(bad, 0.0, f)
        fkt[n] = f
        fkb[n] = nt(eye, f.astype(BF)).astype(BF)

    for n in range(1, NB):
        key_chunk(n)
    fkx = nt(eye, halves(nt(w2k, edges(kbuf))).astype(BF)).astype(BF)
    arrived(1)
    halo(1, go)

    def value_chunk(n):
        va = jnp.concatenate([nt(eye, vbuf[pl.ds(n * CH, CH)]), one_row], axis=0).astype(BF)
        vta[n] = va
        return nn(va, fkb[n])

    vax = jnp.concatenate([nt(eye, edges(vbuf)), one_row], axis=0).astype(BF)
    head_sum = nn(vax[:, :WIN], fkx[:WIN])
    run = head_sum
    for n in range(1, NB):
        pre[n] = run
        run = run + value_chunk(n)
    own1[...] = split(run + nn(vax[:, WIN:], fkx[WIN:]))
    vta[NB, :, pl.ds(0, WIN)] = jnp.concatenate(
        [nt(eye, vbuf[pl.ds(NB * CH, WIN)]), one_row[:, :WIN]], axis=0).astype(BF)

    def scan_copy(o, own, got, recv):
        return pltpu.make_async_remote_copy(
            own, got.at[b], a_send, recv, device_id=ctx(place(lax.rem(b + o, NB), h)),
            device_id_type=MESH)

    def forward(o, act):
        @pl.when(b + o < NB)
        def _():
            act(scan_copy(o, own1, ag1, a1_recv))

    def backward(o, act):
        @pl.when(b - o >= 0)
        def _():
            act(scan_copy(NB - o, own2, ag2, a2_recv))

    for o in range(7, 0, -1):
        forward(o, go)

    @pl.when(b > 0)
    def _():
        for a in range(2):
            part = arrays[a][1].at[pl.ds(0, WIN)]
            pltpu.make_async_copy(part, part, h_recv.at[a]).wait()

    key_chunk(0)
    pre[0] = head_sum - value_chunk(0)

    arrived(2)
    scale = 1.0 / HD**0.5

    def query_chunk(n):
        q = qbuf[pl.ds(n * CH, CH)]
        f = halves(nt(w2q, q))
        fqt[n] = f
        fb = f.astype(BF)
        fqb[n] = fb
        sc = nt(kbuf[pl.ds(n * CH, CH + WIN)], q) * scale
        sc = sc + mask[1 if n else 0]
        top = jnp.max(sc, axis=0, keepdims=True)
        w = jnp.exp(sc - top).astype(BF)
        wn = nn(vta[n], w[:CH]) + nn(vta[n + 1, :, pl.ds(0, WIN)], w[CH:])
        ws = jnp.exp(jnp.minimum(top, 0.0))
        ls = jnp.exp(-jnp.maximum(top, 0.0))
        if n == 0:
            early = jnp.logical_and(first_block, lax.broadcasted_iota(jnp.int32, (1, CH), 1) < WIN)
            ws = jnp.where(early, 1.0, ws)
            ls = jnp.where(early, 0.0, ls)
        am = jnp.where(lower, nn(fkb[n], fb), 0.0).astype(BF)
        ln = nn(vta[n], am) + nn(split(pre[n]), fb)
        win[n] = ws * wn + ls * ln
        scal[n] = jnp.broadcast_to(ls, (8, CH))

    each(query_chunk)

    lin[...] = jnp.zeros((AUG, CH), F32)
    for k in range(1, NB):
        @pl.when(b == k)
        def _():
            left(ag1.at[pl.ds(0, k)], a1_recv)

    for m in range(NB - 1):
        @pl.when(m < b)
        def _():
            lin[...] += ag1[m].astype(F32)
    carry = joined(lin[...])
    carry_b = split(carry)

    def out_chunk(n):
        full = win[n] + scal[n][:1] * nn(carry_b, fqb[n])
        inv = 1.0 / full[HD : HD + 1]
        out = full[:HD] * inv
        outs[n] = out
        scal[n] = jnp.broadcast_to(scal[n][:1] * inv, (8, CH))

    each(out_chunk)
    arrived(3)
    errors, suffix = [], [jnp.zeros((AUG, CH), F32)]

    def diff_chunk(k):
        n = NB - 1 - k
        coef, out = scal[n][:1], outs[n]
        diff = out - nt(eye, tbuf[pl.ds(n * CH, CH)])
        sq = diff * diff
        for r in range(HD // 8):
            errors.append(sq[8 * r : 8 * r + 8])
        g = diff * (2.0 / HD)
        gd = -coef * jnp.sum(g * out, axis=0, keepdims=True)
        scal[n] = jnp.broadcast_to(gd, (8, CH))
        ga = jnp.concatenate([coef * g, gd * one_row], axis=0).astype(BF)
        gna[n] = ga
        later[n] = suffix[-1]
        suffix.append(suffix[-1] + nt(ga, fqb[n]))

    each(diff_chunk)
    own2[...] = split(suffix[-1])
    while len(errors) > 1:
        errors = [sum(errors[i : i + 2]) for i in range(0, len(errors), 2)]
    la[b] = errors[0]
    for o in range(7, 0, -1):
        backward(o, go)

    def loss_a(o, act):
        act(pltpu.make_async_remote_copy(
            la.at[b], la.at[b], l_send, l_recv.at[0],
            device_id=ctx(place(lax.rem(b + o, NB), h)), device_id_type=MESH))

    def loss_b(o, act):
        act(pltpu.make_async_remote_copy(
            lb.at[xme], lb.at[xme], l_send, l_recv.at[1],
            device_id={"head": lax.rem(xme + o, 4)}, device_id_type=MESH))

    def loss_c(o, act):
        act(pltpu.make_async_remote_copy(
            lc.at[h], lc.at[h], l_send, l_recv.at[2],
            device_id=ctx(place(b, lax.rem(h + o, NB))), device_id_type=MESH))

    def total(ref, count, level):
        part = ref.at[pl.ds(0, count - 1)]
        pltpu.make_async_copy(part, part, l_recv.at[level]).wait()
        acc = ref[0]
        for m in range(1, count):
            acc = acc + ref[m]
        return acc

    for o in range(1, NB):
        loss_a(o, go)

    def student(j, act):
        to = NB * b + j

        def remote():
            act(pltpu.make_async_remote_copy(
                stu.at[j], stu_got.at[h], s_send, s_recv, device_id=ctx(to), device_id_type=MESH))

        pl.when(to != me)(remote)
        if act is go:
            @pl.when(to == me)
            def _():
                pltpu.make_async_copy(stu.at[j], stu_got.at[h], s_recv).start()

    for j in range(NB):
        stu[j] = nt(eye, outs[j].astype(BF)).astype(BF)
    for j in range(NB):
        student(j, go)

    dq = []

    def mix_chunk(n):
        gd = scal[n][:1]
        ga = gna[n]
        mx = nn(vbuf[pl.ds(n * CH, CH)], ga[:HD]) + gd
        mx = jnp.where(lower, mx, 0.0).astype(BF)
        st = nt(eye, split(pre[n] + carry)).astype(BF)
        gq = nn(fkt[n].astype(BF), mx) + nn(st, ga)
        dq.append(proj_grad(fqt[n], gq))
        lt = nt(eye, split(later[n])).astype(BF)
        gfk[n] = nt(fqb[n], mx) + nn(lt, vta[n])

    each(mix_chunk)
    gpart[0] = nn(jnp.concatenate(dq, axis=1), qbuf[...]).astype(BF)

    def half(core):
        return pl.ds(pl.multiple_of(HF // 2 * core, HF // 2), HF // 2)

    def share(w, o, act):
        m = lax.rem(b + o, NB)
        act(pltpu.make_async_remote_copy(
            gpart.at[w, half(lax.rem(m, 2))], gsum.at[w, b], r_send, r_recv.at[w],
            device_id=ctx(place(m, h)), device_id_type=MESH))

    def summed(w):
        gsum[w, b] = gpart[w, half(c)]
        part = gsum.at[w, pl.ds(0, NB - 1)]
        pltpu.make_async_copy(part, part, r_recv.at[w]).wait()
        acc = gsum[w, 0].astype(F32)
        for m in range(1, NB):
            acc = acc + gsum[w, m].astype(F32)
        fin[w] = acc.astype(BF)

    def spread(w, o, act):
        act(pltpu.make_async_remote_copy(
            fin.at[w], fin_out.at[w, h, half(c)], f_send, f_recv.at[w, o],
            device_id=ctx(place(b, lax.rem(h + o, NB))), device_id_type=MESH))

    def partner(w, src, head):
        pltpu.make_async_remote_copy(
            src, fin_out.at[w, head, half(c)], g_send, g_recv,
            device_id=ctx(me + 1 - 2 * c), device_id_type=MESH).start()

    def spread_all(w):
        for o in FAR[:-1]:
            spread(w, o, go)
        pltpu.make_async_copy(fin.at[w], fin_out.at[w, h, half(c)], f_recv.at[w, 0]).start()
        partner(w, fin.at[w], h)

    def pass_on(w):
        for o in reversed(FAR[:-1]):
            head = lax.rem(h - o + NB, NB)
            mine = fin_out.at[w, head, half(c)]
            pltpu.make_async_copy(mine, mine, f_recv.at[w, o]).wait()
            partner(w, mine, head)

    for o in range(1, NB):
        share(0, o, go)
    lb[xme] = total(la, NB, 0)
    for o in range(1, 4):
        loss_b(o, go)

    lin[...] = jnp.zeros((AUG, CH), F32)
    for k in range(1, NB):
        @pl.when(b == NB - 1 - k)
        def _():
            left(ag2.at[pl.ds(NB - k, k)], a2_recv)

    for m in range(1, NB):
        @pl.when(m > b)
        def _():
            lin[...] += ag2[m].astype(F32)
    after = nt(eye, split(joined(lin[...]))).astype(BF)
    dk = []

    def key_grad(n):
        dk.append(proj_grad(fkt[n], gfk[n] + nn(after, vta[n])))

    each(key_grad)
    gpart[1] = nn(jnp.concatenate(dk, axis=1), kbuf[pl.ds(0, NB * CH)]).astype(BF)
    for o in range(1, NB):
        share(1, o, go)
    summed(0)
    spread_all(0)
    lc[h] = total(lb, 4, 1)
    for o in range(1, NB):
        loss_c(o, go)
    summed(1)
    spread_all(1)

    pltpu.make_async_copy(stu_got, stu_got, s_recv).wait()
    stu_t[...] = jnp.swapaxes(stu_got[...], 0, 1)
    put = pltpu.make_async_copy(stu_t, stu_out, out_sem)
    put.start()
    pass_on(0)
    pass_on(1)

    own = (me == place(src_b, h)).astype(jnp.int32)
    for n in range(2):
        @pl.when(own == n)
        def _():
            left(xs.at[:, pl.ds(0, NB - n)], x_send)
            left(stu.at[pl.ds(0, NB - n)], s_send)

    for a in range(2):
        halo(a, sent)
    left(ag1.at[pl.ds(0, NB - 1)], a_send)
    left(win.at[0, pl.ds(0, 8 * 17)], l_send)
    left(gsum.at[:, pl.ds(0, NB - 1)], r_send)
    left(gsum.at[:, pl.ds(0, NB - 1)], f_send)
    loss[...] = jnp.sum(total(lc, NB, 2), keepdims=True) * (1.0 / (8192 * 32 * 128))
    put_loss = pltpu.make_async_copy(loss, loss_out, loss_sem)
    put_loss.start()
    put.wait()
    put_loss.wait()
    for w in range(2):
        left(fin.at[w], f_recv.at[w, 0])
    left(gsum, g_send)
    left(gsum, g_recv)


def finish(stu_in, fin_in, loss_in, stu_out, gq_out, gk_out, loss_out, fin, gq, gk, loss, in_sem, out_sem):
    loads = [
        pltpu.make_async_copy(src, dst, in_sem.at[i])
        for i, (src, dst) in enumerate(((fin_in, fin), (loss_in, loss)))
    ]
    stores = [
        pltpu.make_async_copy(src, dst, out_sem.at[i])
        for i, (src, dst) in enumerate(((gq, gq_out), (gk, gk_out), (loss, loss_out), (stu_in, stu_out)))
    ]
    for load in loads:
        load.start()
    stores[3].start()
    loads[0].wait()
    gq[...] = fin[0].astype(F32)
    stores[0].start()
    gk[...] = fin[1].astype(F32)
    stores[1].start()
    loads[1].wait()
    stores[2].start()
    for store in stores:
        store.wait()


def per_device(queries, keys, values, teacher, wq, wk):
    anywhere = pl.BlockSpec(memory_space=pl.ANY)
    dma = pltpu.SemaphoreType.DMA
    stu, fin, loss = pl.pallas_call(
        kernel,
        out_shape=(
            jax.ShapeDtypeStruct((CH, NB, HD), BF),
            jax.ShapeDtypeStruct((2, NB, HF, HD), BF),
            jax.ShapeDtypeStruct((1, 1), F32),
        ),
        in_specs=[anywhere] * 6,
        out_specs=(anywhere,) * 3,
        scratch_shapes=[
            pltpu.VMEM((4, CH, NB, HD), BF),
            pltpu.VMEM((4, NB, CH, HD), BF),
            pltpu.VMEM((NB, HF, HD), BF),
            pltpu.VMEM((NB, HF, HD), BF),
            pltpu.VMEM((NB * CH + WIN, HD), BF),
            pltpu.VMEM((NB * CH + WIN, HD), BF),
            pltpu.VMEM((NB * CH, HD), BF),
            pltpu.VMEM((NB * CH, HD), BF),
            pltpu.VMEM((NB, CH, CH), F32),
            pltpu.VMEM((NB, CH, CH), BF),
            pltpu.VMEM((NB, CH, CH), F32),
            pltpu.VMEM((NB, CH, CH), BF),
            pltpu.VMEM((NB + 1, AUG, CH), BF),
            pltpu.VMEM((NB, AUG, CH), F32),
            pltpu.VMEM((NB, AUG, CH), F32),
            pltpu.VMEM((NB, HD, CH), F32),
            pltpu.VMEM((AUG, CH), F32),
            pltpu.VMEM((NB, AUG, CH), BF),
            pltpu.VMEM((NB, CH, CH), F32),
            pltpu.VMEM((NB, AUG, CH), F32),
            pltpu.VMEM((AUG, CH), BF),
            pltpu.VMEM((NB, AUG, CH), BF),
            pltpu.VMEM((AUG, CH), BF),
            pltpu.VMEM((NB, AUG, CH), BF),
            pltpu.VMEM((NB, CH, HD), BF),
            pltpu.VMEM((NB, CH, HD), BF),
            pltpu.VMEM((CH, NB, HD), BF),
            pltpu.VMEM((2, HF, HD), BF),
            pltpu.VMEM((2, NB, HF // 2, HD), BF),
            pltpu.VMEM((2, HF // 2, HD), BF),
            pltpu.VMEM((NB, 8, CH), F32),
            pltpu.VMEM((4, 8, CH), F32),
            pltpu.VMEM((NB, 8, CH), F32),
            pltpu.VMEM((1, 1), F32),
            pltpu.VMEM((NB, 8, CH), F32),
            pltpu.VMEM((2, CH + WIN, CH), F32),
            dma((4,)), dma((2,)), dma, dma,
            dma, dma((4,)),
            dma((2,)), dma((2,)),
            dma, dma, dma,
            dma, dma,
            dma, dma((2,)),
            dma, dma((2, NB)),
            dma, dma,
            dma, dma((3,)),
        ],
        compiler_params=pltpu.CompilerParams(
            collective_id=0, has_side_effects=True, vmem_limit_bytes=24 * 2**20),
    )(*(pltpu.with_memory_space_constraint(x, pltpu.HBM) for x in (queries, keys, values, teacher, wq, wk)))
    stu, gq, gk, loss = pl.pallas_call(
        finish,
        out_shape=(
            jax.ShapeDtypeStruct((CH, NB, HD), BF),
            jax.ShapeDtypeStruct((NB, HF, HD), F32),
            jax.ShapeDtypeStruct((NB, HF, HD), F32),
            jax.ShapeDtypeStruct((1, 1), F32),
        ),
        in_specs=[anywhere] * 3,
        out_specs=(anywhere,) * 4,
        scratch_shapes=[
            pltpu.VMEM((2, NB, HF, HD), BF),
            pltpu.VMEM((NB, HF, HD), F32),
            pltpu.VMEM((NB, HF, HD), F32),
            pltpu.VMEM((1, 1), F32),
            dma((2,)),
            dma((4,)),
        ],
        compiler_params=pltpu.CompilerParams(vmem_limit_bytes=8 * 2**20),
    )(stu, fin, loss)
    return stu, loss[0, 0], gq, gk


def solution(mesh):
    tok = P("ctx", "head", None)
    par = P("head", None, None)
    return jax.shard_map(
        per_device,
        mesh=mesh,
        in_specs=(tok, tok, tok, tok, par, par),
        out_specs=(tok, P(), par, par),
        check_vma=False,
    )
```

```python
import jax
import jax.numpy as jnp
from jax import lax
from jax.experimental import pallas as pl
from jax.experimental.pallas import tpu as pltpu
from jax.sharding import PartitionSpec as P

NB = 8
CH = 128
WIN = 64
HD = 128
HF = 64
AUG = 144
FAR = (4, 3, 5, 2, 6, 1, 7, 0)
MESH = pl.DeviceIdType.MESH
BF = jnp.bfloat16
F32 = jnp.float32


def nt(a, b):
    return lax.dot_general(a, b, (((1,), (1,)), ((), ())), preferred_element_type=F32)


def nn(a, b):
    return jnp.dot(a, b, preferred_element_type=F32)


def halves(proj):
    e = []
    for s in (proj[:HF], proj[HF:]):
        w = jnp.exp(s - jnp.max(s, axis=0, keepdims=True))
        e.append(w * (1.0 / jnp.sum(w, axis=0, keepdims=True)))
    return jnp.concatenate(e, axis=0)


def proj_grad(feat, grad):
    d = []
    for a in (0, HF):
        u, g = feat[a : a + HF], grad[a : a + HF]
        d.append(u * (g - jnp.sum(u * g, axis=0, keepdims=True)))
    return (d[0] - d[1]).astype(BF)


def split(x):
    norm = x[HD : HD + 1]
    high = norm.astype(BF).astype(F32)
    row = lax.broadcasted_iota(jnp.int32, (AUG - HD, CH), 0)
    aug = jnp.where(row == 0, high, jnp.where(row == 1, norm - high, 0.0))
    return jnp.concatenate([x[:HD], aug], axis=0).astype(BF)


def joined(x):
    return jnp.concatenate([x[:HD], x[HD : HD + 8] + pltpu.roll(x[HD : HD + 8], 7, 0), x[HD + 8 :]], axis=0)


def place(block, head):
    return 16 * (block // 2) + 2 * head + lax.rem(block, 2)


def each(body):
    for n in range(NB):
        body(n)


def kernel(
    q_hbm, k_hbm, v_hbm, t_hbm, wq_hbm, wk_hbm,
    stu_out, fin_out, loss_out,
    xin, xs, wq_ref, wk_ref,
    kbuf, vbuf, qbuf, tbuf, fkt, fkb, fqt, fqb, vta, pre, win, outs, diffs, lin, gna, gfk, later,
    own1, ag1, own2, ag2, stu, stu_got, stu_t, gpart, gsum, fin, la, lb, lc, scal, mask,
    in_sem, w_sem, out_sem,
    x_send, x_recv, h_send, h_recv, a_send, a1_recv, a2_recv,
    s_send, s_recv, r_send, r_recv, f_send, f_recv, g_send, g_recv, l_send, l_recv,
):
    me = lax.axis_index("ctx")
    xme = lax.axis_index("head")
    src_b, src_j = me // NB, lax.rem(me, NB)
    b = 2 * (me // 16) + lax.rem(me, 2)
    h = lax.rem(me, 16) // 2
    first_block = b == 0

    def ctx(i):
        return {"ctx": i}

    y, z, c = me // 16, h, lax.rem(me, 2)
    k_in, v_in, q_in, t_in = (xs.at[a] for a in range(4))
    loads = [pltpu.make_async_copy(src, xin.at[a], in_sem.at[a]) for a, src in enumerate((k_hbm, v_hbm, q_hbm, t_hbm))]
    weights = [
        pltpu.make_async_copy(wq_hbm, wq_ref, w_sem.at[0]),
        pltpu.make_async_copy(wk_hbm, wk_ref, w_sem.at[1]),
    ]

    bar = pltpu.get_barrier_semaphore()

    def greet(device):
        pl.semaphore_signal(bar, inc=1, device_id=device, device_id_type=MESH)

    for o in FAR:
        for d in range(2):
            if o or d:
                greet(ctx(16 * y + 2 * lax.rem(z + o, NB) + lax.rem(c + d, 2)))
    for o in range(1, 4):
        for d in range(2):
            greet(ctx(16 * lax.rem(y + o, 4) + 2 * z + d))
        greet({"head": lax.rem(xme + o, 4)})
    for load in loads + weights:
        load.start()
    for a in range(4):
        loads[a].wait()
        xs[a] = jnp.swapaxes(xin[a], 0, 1)
    for load in weights:
        load.wait()
    pl.semaphore_wait(bar, 24)

    arrays = ((k_in, kbuf, WIN), (v_in, vbuf, WIN), (q_in, qbuf, 0), (t_in, tbuf, 0))

    def exchange(a, o, act):
        src, dst, base = arrays[a]
        hd = lax.rem(h + o, NB)
        to = place(src_b, hd)
        rows = dst.at[pl.ds(pl.multiple_of(base + CH * src_j, WIN), CH)]

        def remote():
            act(pltpu.make_async_remote_copy(
                src.at[hd], rows, x_send, x_recv.at[a], device_id=ctx(to), device_id_type=MESH))

        if o == 0:
            pl.when(to != me)(remote)
            if act is go:
                @pl.when(to == me)
                def _():
                    pltpu.make_async_copy(src.at[hd], rows, x_recv.at[a]).start()
        else:
            remote()

    def left(ref, sem):
        pltpu.make_async_copy(ref, ref, sem).wait()

    def go(c):
        c.start()

    def sent(c):
        c.wait_send()

    def halo(a, act):
        dst = arrays[a][1]

        @pl.when(b < NB - 1)
        def _():
            act(pltpu.make_async_remote_copy(
                dst.at[pl.ds(NB * CH, WIN)], dst.at[pl.ds(0, WIN)], h_send.at[a], h_recv.at[a],
                device_id=ctx(place(b + 1, h)), device_id_type=MESH))

    for a in range(4):
        for o in FAR:
            exchange(a, o, go)

    @pl.when(first_block)
    def _():
        kbuf[pl.ds(0, WIN)] = jnp.zeros((WIN, HD), BF)
        vbuf[pl.ds(0, WIN)] = jnp.zeros((WIN, HD), BF)

    ci = lax.broadcasted_iota(jnp.int32, (CH + WIN, CH), 0)
    ii = lax.broadcasted_iota(jnp.int32, (CH + WIN, CH), 1)
    inwin = jnp.logical_and(ci > ii, ci <= ii + WIN)
    mask[0] = jnp.where(jnp.logical_and(inwin, jnp.logical_or(ci >= WIN, b > 0)), 0.0, -jnp.inf)
    mask[1] = jnp.where(inwin, 0.0, -jnp.inf)
    eye = jnp.where(
        lax.broadcasted_iota(jnp.int32, (CH, CH), 0) == lax.broadcasted_iota(jnp.int32, (CH, CH), 1),
        1.0, 0.0).astype(BF)
    one_row = jnp.where(lax.broadcasted_iota(jnp.int32, (AUG - HD, CH), 0) < 2, 1.0, 0.0)
    wq1, wk1 = wq_ref[h], wk_ref[h]
    w2q = jnp.concatenate([wq1, -wq1], axis=0)
    w2k = jnp.concatenate([wk1, -wk1], axis=0)

    def arrived(a):
        src, dst, base = arrays[a]
        part = dst.at[pl.ds(base, NB * CH)]
        pltpu.make_async_copy(part, part, x_recv.at[a]).wait()

    arrived(0)
    halo(0, go)

    cidx = lax.broadcasted_iota(jnp.int32, (CH, CH), 0)
    iidx = lax.broadcasted_iota(jnp.int32, (CH, CH), 1)
    lower = cidx <= iidx

    def edges(buf):
        return jnp.concatenate([buf[pl.ds(WIN, WIN)], buf[pl.ds(NB * CH, WIN)]], axis=0)

    def key_chunk(n):
        f = halves(nt(w2k, kbuf[pl.ds(n * CH, CH)]))
        if n == 0:
            bad = jnp.logical_and(first_block, iidx < WIN)
            f = jnp.where(bad, 0.0, f)
        fkt[n] = f
        fkb[n] = nt(eye, f.astype(BF)).astype(BF)

    for n in range(1, NB):
        key_chunk(n)
    fkx = nt(eye, halves(nt(w2k, edges(kbuf))).astype(BF)).astype(BF)
    arrived(1)
    halo(1, go)

    def value_chunk(n):
        va = jnp.concatenate([nt(eye, vbuf[pl.ds(n * CH, CH)]), one_row], axis=0).astype(BF)
        vta[n] = va
        return nn(va, fkb[n])

    vax = jnp.concatenate([nt(eye, edges(vbuf)), one_row], axis=0).astype(BF)
    head_sum = nn(vax[:, :WIN], fkx[:WIN])
    run = head_sum
    for n in range(1, NB):
        pre[n] = run
        run = run + value_chunk(n)
    own1[...] = split(run + nn(vax[:, WIN:], fkx[WIN:]))
    vta[NB, :, pl.ds(0, WIN)] = jnp.concatenate(
        [nt(eye, vbuf[pl.ds(NB * CH, WIN)]), one_row[:, :WIN]], axis=0).astype(BF)

    def scan_copy(o, own, got, recv):
        return pltpu.make_async_remote_copy(
            own, got.at[b], a_send, recv, device_id=ctx(place(lax.rem(b + o, NB), h)),
            device_id_type=MESH)

    def forward(o, act):
        @pl.when(b + o < NB)
        def _():
            act(scan_copy(o, own1, ag1, a1_recv))

    def backward(o, act):
        @pl.when(b - o >= 0)
        def _():
            act(scan_copy(NB - o, own2, ag2, a2_recv))

    for o in range(7, 0, -1):
        forward(o, go)

    @pl.when(b > 0)
    def _():
        for a in range(2):
            part = arrays[a][1].at[pl.ds(0, WIN)]
            pltpu.make_async_copy(part, part, h_recv.at[a]).wait()

    key_chunk(0)
    pre[0] = head_sum - value_chunk(0)

    arrived(2)
    scale = 1.0 / HD**0.5

    def query_chunk(n):
        q = qbuf[pl.ds(n * CH, CH)]
        f = halves(nt(w2q, q))
        fqt[n] = f
        fb = f.astype(BF)
        fqb[n] = fb
        sc = nt(kbuf[pl.ds(n * CH, CH + WIN)], q) * scale
        sc = sc + mask[1 if n else 0]
        top = jnp.max(sc, axis=0, keepdims=True)
        w = jnp.exp(sc - top).astype(BF)
        wn = nn(vta[n], w[:CH]) + nn(vta[n + 1, :, pl.ds(0, WIN)], w[CH:])
        ws = jnp.exp(jnp.minimum(top, 0.0))
        ls = jnp.exp(-jnp.maximum(top, 0.0))
        if n == 0:
            early = jnp.logical_and(first_block, lax.broadcasted_iota(jnp.int32, (1, CH), 1) < WIN)
            ws = jnp.where(early, 1.0, ws)
            ls = jnp.where(early, 0.0, ls)
        am = jnp.where(lower, nn(fkb[n], fb), 0.0).astype(BF)
        ln = nn(vta[n], am) + nn(split(pre[n]), fb)
        win[n] = ws * wn + ls * ln
        scal[n] = jnp.broadcast_to(ls, (8, CH))

    each(query_chunk)

    lin[...] = jnp.zeros((AUG, CH), F32)
    for k in range(1, NB):
        @pl.when(b == k)
        def _():
            left(ag1.at[pl.ds(0, k)], a1_recv)

    for m in range(NB - 1):
        @pl.when(m < b)
        def _():
            lin[...] += ag1[m].astype(F32)
    carry = joined(lin[...])
    carry_b = split(carry)

    def out_chunk(n):
        full = win[n] + scal[n][:1] * nn(carry_b, fqb[n])
        inv = 1.0 / full[HD : HD + 1]
        out = full[:HD] * inv
        outs[n] = out
        scal[n] = jnp.broadcast_to(scal[n][:1] * inv, (8, CH))

    each(out_chunk)
    arrived(3)
    suffix = [jnp.zeros((AUG, CH), F32)]

    def diff_chunk(k):
        n = NB - 1 - k
        coef, out = scal[n][:1], outs[n]
        diff = out - nt(eye, tbuf[pl.ds(n * CH, CH)])
        g = diff * (2.0 / HD)
        gd = -coef * jnp.sum(g * out, axis=0, keepdims=True)
        scal[n] = jnp.broadcast_to(gd, (8, CH))
        diffs[n] = diff
        ga = jnp.concatenate([coef * g, gd * one_row], axis=0).astype(BF)
        gna[n] = ga
        later[n] = suffix[-1]
        suffix.append(suffix[-1] + nt(ga, fqb[n]))

    each(diff_chunk)
    own2[...] = split(suffix[-1])
    for o in range(7, 0, -1):
        backward(o, go)
    errors = []
    for n in range(NB):
        sq = diffs[n] * diffs[n]
        for r in range(HD // 8):
            errors.append(sq[8 * r : 8 * r + 8])
    while len(errors) > 1:
        errors = [sum(errors[i : i + 2]) for i in range(0, len(errors), 2)]
    la[b] = errors[0]

    def loss_a(o, act):
        act(pltpu.make_async_remote_copy(
            la.at[b], la.at[b], l_send, l_recv.at[0],
            device_id=ctx(place(lax.rem(b + o, NB), h)), device_id_type=MESH))

    def loss_b(o, act):
        act(pltpu.make_async_remote_copy(
            lb.at[xme], lb.at[xme], l_send, l_recv.at[1],
            device_id={"head": lax.rem(xme + o, 4)}, device_id_type=MESH))

    def loss_c(o, act):
        act(pltpu.make_async_remote_copy(
            lc, loss_out.at[h], l_send, l_recv.at[2],
            device_id=ctx(place(b, lax.rem(h + o, NB))), device_id_type=MESH))

    def total(ref, count, level):
        part = ref.at[pl.ds(0, count - 1)]
        pltpu.make_async_copy(part, part, l_recv.at[level]).wait()
        acc = ref[0]
        for m in range(1, count):
            acc = acc + ref[m]
        return acc

    for o in range(1, NB):
        loss_a(o, go)

    def student(j, act):
        to = NB * b + j

        def remote():
            act(pltpu.make_async_remote_copy(
                stu.at[j], stu_got.at[h], s_send, s_recv, device_id=ctx(to), device_id_type=MESH))

        pl.when(to != me)(remote)
        if act is go:
            @pl.when(to == me)
            def _():
                pltpu.make_async_copy(stu.at[j], stu_got.at[h], s_recv).start()

    for j in range(NB):
        stu[j] = nt(eye, outs[j].astype(BF)).astype(BF)
    for j in range(NB):
        student(j, go)

    dq = []

    def mix_chunk(n):
        gd = scal[n][:1]
        ga = gna[n]
        mx = nn(vbuf[pl.ds(n * CH, CH)], ga[:HD]) + gd
        mx = jnp.where(lower, mx, 0.0).astype(BF)
        st = nt(eye, split(pre[n] + carry)).astype(BF)
        gq = nn(fkt[n].astype(BF), mx) + nn(st, ga)
        dq.append(proj_grad(fqt[n], gq))
        lt = nt(eye, split(later[n])).astype(BF)
        gfk[n] = nt(fqb[n], mx) + nn(lt, vta[n])

    each(mix_chunk)
    gpart[0] = nn(jnp.concatenate(dq, axis=1), qbuf[...]).astype(BF)

    def half(core):
        return pl.ds(pl.multiple_of(HF // 2 * core, HF // 2), HF // 2)

    def share(w, o, act):
        m = lax.rem(b + o, NB)
        act(pltpu.make_async_remote_copy(
            gpart.at[w, half(lax.rem(m, 2))], gsum.at[w, b], r_send, r_recv.at[w],
            device_id=ctx(place(m, h)), device_id_type=MESH))

    def summed(w):
        gsum[w, b] = gpart[w, half(c)]
        part = gsum.at[w, pl.ds(0, NB - 1)]
        pltpu.make_async_copy(part, part, r_recv.at[w]).wait()
        acc = gsum[w, 0].astype(F32)
        for m in range(1, NB):
            acc = acc + gsum[w, m].astype(F32)
        fin[w] = acc.astype(BF)

    def spread(w, o, act):
        act(pltpu.make_async_remote_copy(
            fin.at[w], fin_out.at[w, h, half(c)], f_send, f_recv.at[w, o],
            device_id=ctx(place(b, lax.rem(h + o, NB))), device_id_type=MESH))

    def partner(w, src, head):
        pltpu.make_async_remote_copy(
            src, fin_out.at[w, head, half(c)], g_send, g_recv,
            device_id=ctx(me + 1 - 2 * c), device_id_type=MESH).start()

    def spread_all(w):
        for o in FAR[:-1]:
            spread(w, o, go)
        pltpu.make_async_copy(fin.at[w], fin_out.at[w, h, half(c)], f_recv.at[w, 0]).start()
        partner(w, fin.at[w], h)

    def pass_on(w):
        for o in reversed(FAR[:-1]):
            head = lax.rem(h - o + NB, NB)
            mine = fin_out.at[w, head, half(c)]
            pltpu.make_async_copy(mine, mine, f_recv.at[w, o]).wait()
            partner(w, mine, head)

    for o in range(1, NB):
        share(0, o, go)
    lb[xme] = total(la, NB, 0)
    for o in range(1, 4):
        loss_b(o, go)

    lin[...] = jnp.zeros((AUG, CH), F32)
    for k in range(1, NB):
        @pl.when(b == NB - 1 - k)
        def _():
            left(ag2.at[pl.ds(NB - k, k)], a2_recv)

    for m in range(1, NB):
        @pl.when(m > b)
        def _():
            lin[...] += ag2[m].astype(F32)
    after = nt(eye, split(joined(lin[...]))).astype(BF)
    dk = []

    def key_grad(n):
        dk.append(proj_grad(fkt[n], gfk[n] + nn(after, vta[n])))

    each(key_grad)
    gpart[1] = nn(jnp.concatenate(dk, axis=1), kbuf[pl.ds(0, NB * CH)]).astype(BF)
    for o in range(1, NB):
        share(1, o, go)
    summed(0)
    spread_all(0)
    summed(1)
    spread_all(1)
    lc[...] = total(lb, 4, 1)
    for o in range(1, NB):
        loss_c(o, go)
    pltpu.make_async_copy(lc, loss_out.at[h], l_recv.at[2]).start()

    pltpu.make_async_copy(stu_got, stu_got, s_recv).wait()
    stu_t[...] = jnp.swapaxes(stu_got[...], 0, 1)
    put = pltpu.make_async_copy(stu_t, stu_out, out_sem)
    put.start()
    pass_on(0)
    pass_on(1)

    own = (me == place(src_b, h)).astype(jnp.int32)
    for n in range(2):
        @pl.when(own == n)
        def _():
            left(xs.at[:, pl.ds(0, NB - n)], x_send)
            left(stu.at[pl.ds(0, NB - n)], s_send)

    for a in range(2):
        halo(a, sent)
    left(ag1.at[pl.ds(0, NB - 1)], a_send)
    left(win.at[0, pl.ds(0, 8 * 17)], l_send)
    left(gsum.at[:, pl.ds(0, NB - 1)], r_send)
    left(gsum.at[:, pl.ds(0, NB - 1)], f_send)
    put.wait()
    left(loss_out, l_recv.at[2])
    for w in range(2):
        left(fin.at[w], f_recv.at[w, 0])
    left(gsum, g_send)
    left(gsum, g_recv)


def finish(stu_in, fin_in, loss_in, stu_out, gq_out, gk_out, loss_out, fin, gq, gk, parts, loss, in_sem, out_sem):
    loads = [
        pltpu.make_async_copy(src, dst, in_sem.at[i])
        for i, (src, dst) in enumerate(((fin_in.at[0], fin.at[0]), (fin_in.at[1], fin.at[1]), (loss_in, parts)))
    ]
    stores = [
        pltpu.make_async_copy(src, dst, out_sem.at[i])
        for i, (src, dst) in enumerate(((gq, gq_out), (gk, gk_out), (loss, loss_out), (stu_in, stu_out)))
    ]
    for load in loads:
        load.start()
    stores[3].start()
    loads[0].wait()
    gq[...] = fin[0].astype(F32)
    stores[0].start()
    loads[1].wait()
    gk[...] = fin[1].astype(F32)
    stores[1].start()
    loads[2].wait()
    loss[...] = jnp.sum(parts[...], keepdims=True)[0] * (1.0 / (8192 * 32 * 128))
    stores[2].start()
    for store in stores:
        store.wait()


def per_device(queries, keys, values, teacher, wq, wk):
    anywhere = pl.BlockSpec(memory_space=pl.ANY)
    dma = pltpu.SemaphoreType.DMA
    stu, fin, loss = pl.pallas_call(
        kernel,
        out_shape=(
            jax.ShapeDtypeStruct((CH, NB, HD), BF),
            jax.ShapeDtypeStruct((2, NB, HF, HD), BF),
            jax.ShapeDtypeStruct((NB, 8, CH), F32),
        ),
        in_specs=[anywhere] * 6,
        out_specs=(anywhere,) * 3,
        scratch_shapes=[
            pltpu.VMEM((4, CH, NB, HD), BF),
            pltpu.VMEM((4, NB, CH, HD), BF),
            pltpu.VMEM((NB, HF, HD), BF),
            pltpu.VMEM((NB, HF, HD), BF),
            pltpu.VMEM((NB * CH + WIN, HD), BF),
            pltpu.VMEM((NB * CH + WIN, HD), BF),
            pltpu.VMEM((NB * CH, HD), BF),
            pltpu.VMEM((NB * CH, HD), BF),
            pltpu.VMEM((NB, CH, CH), F32),
            pltpu.VMEM((NB, CH, CH), BF),
            pltpu.VMEM((NB, CH, CH), F32),
            pltpu.VMEM((NB, CH, CH), BF),
            pltpu.VMEM((NB + 1, AUG, CH), BF),
            pltpu.VMEM((NB, AUG, CH), F32),
            pltpu.VMEM((NB, AUG, CH), F32),
            pltpu.VMEM((NB, HD, CH), F32),
            pltpu.VMEM((NB, HD, CH), F32),
            pltpu.VMEM((AUG, CH), F32),
            pltpu.VMEM((NB, AUG, CH), BF),
            pltpu.VMEM((NB, CH, CH), F32),
            pltpu.VMEM((NB, AUG, CH), F32),
            pltpu.VMEM((AUG, CH), BF),
            pltpu.VMEM((NB, AUG, CH), BF),
            pltpu.VMEM((AUG, CH), BF),
            pltpu.VMEM((NB, AUG, CH), BF),
            pltpu.VMEM((NB, CH, HD), BF),
            pltpu.VMEM((NB, CH, HD), BF),
            pltpu.VMEM((CH, NB, HD), BF),
            pltpu.VMEM((2, HF, HD), BF),
            pltpu.VMEM((2, NB, HF // 2, HD), BF),
            pltpu.VMEM((2, HF // 2, HD), BF),
            pltpu.VMEM((NB, 8, CH), F32),
            pltpu.VMEM((4, 8, CH), F32),
            pltpu.VMEM((8, CH), F32),
            pltpu.VMEM((NB, 8, CH), F32),
            pltpu.VMEM((2, CH + WIN, CH), F32),
            dma((4,)), dma((2,)), dma,
            dma, dma((4,)),
            dma((2,)), dma((2,)),
            dma, dma, dma,
            dma, dma,
            dma, dma((2,)),
            dma, dma((2, NB)),
            dma, dma,
            dma, dma((3,)),
        ],
        compiler_params=pltpu.CompilerParams(
            collective_id=0, has_side_effects=True, vmem_limit_bytes=24 * 2**20),
    )(*(pltpu.with_memory_space_constraint(x, pltpu.HBM) for x in (queries, keys, values, teacher, wq, wk)))
    stu, gq, gk, loss = pl.pallas_call(
        finish,
        out_shape=(
            jax.ShapeDtypeStruct((CH, NB, HD), BF),
            jax.ShapeDtypeStruct((NB, HF, HD), F32),
            jax.ShapeDtypeStruct((NB, HF, HD), F32),
            jax.ShapeDtypeStruct((1, 1), F32),
        ),
        in_specs=[anywhere] * 3,
        out_specs=(anywhere,) * 4,
        scratch_shapes=[
            pltpu.VMEM((2, NB, HF, HD), BF),
            pltpu.VMEM((NB, HF, HD), F32),
            pltpu.VMEM((NB, HF, HD), F32),
            pltpu.VMEM((NB, 8, CH), F32),
            pltpu.VMEM((1, 1), F32),
            dma((3,)),
            dma((4,)),
        ],
        compiler_params=pltpu.CompilerParams(vmem_limit_bytes=8 * 2**20),
    )(stu, fin, loss)
    return stu, loss[0, 0], gq, gk


def solution(mesh):
    tok = P("ctx", "head", None)
    par = P("head", None, None)
    return jax.shard_map(
        per_device,
        mesh=mesh,
        in_specs=(tok, tok, tok, tok, par, par),
        out_specs=(tok, P(), par, par),
        check_vma=False,
    )
```

```python
import jax
import jax.numpy as jnp
from jax import lax
from jax.experimental import pallas as pl
from jax.experimental.pallas import tpu as pltpu
from jax.sharding import PartitionSpec as P

NB = 8
CH = 128
WIN = 64
HD = 128
HF = 64
AUG = 144
FAR = (4, 3, 5, 2, 6, 1, 7, 0)
MESH = pl.DeviceIdType.MESH
BF = jnp.bfloat16
F32 = jnp.float32


def nt(a, b):
    return lax.dot_general(a, b, (((1,), (1,)), ((), ())), preferred_element_type=F32)


def nn(a, b):
    return jnp.dot(a, b, preferred_element_type=F32)


def halves(proj):
    e = []
    for s in (proj[:HF], proj[HF:]):
        w = jnp.exp(s - jnp.max(s, axis=0, keepdims=True))
        e.append(w * (1.0 / jnp.sum(w, axis=0, keepdims=True)))
    return jnp.concatenate(e, axis=0)


def proj_grad(feat, grad):
    d = []
    for a in (0, HF):
        u, g = feat[a : a + HF], grad[a : a + HF]
        d.append(u * (g - jnp.sum(u * g, axis=0, keepdims=True)))
    return (d[0] - d[1]).astype(BF)


def split(x):
    norm = x[HD : HD + 1]
    high = norm.astype(BF).astype(F32)
    row = lax.broadcasted_iota(jnp.int32, (AUG - HD, CH), 0)
    aug = jnp.where(row == 0, high, jnp.where(row == 1, norm - high, 0.0))
    return jnp.concatenate([x[:HD], aug], axis=0).astype(BF)


def joined(x):
    return jnp.concatenate([x[:HD], x[HD : HD + 8] + pltpu.roll(x[HD : HD + 8], 7, 0), x[HD + 8 :]], axis=0)


def place(block, head):
    return 16 * (block // 2) + 2 * head + lax.rem(block, 2)


def each(body):
    for n in range(NB):
        body(n)


def kernel(
    q_hbm, k_hbm, v_hbm, t_hbm, wq_hbm, wk_hbm,
    stu_out, fin_out, loss_out,
    xin, xs, wq_ref, wk_ref,
    kbuf, vbuf, qbuf, tbuf, fkt, fkb, fqt, fqb, vta, pre, win, outs, diffs, lin, gna, gfk, later,
    own1, ag1, own2, ag2, stu, stu_got, stu_t, gpart, gsum, fin, la, lb, lc, scal, mask,
    in_sem, w_sem, out_sem,
    x_send, x_recv, h_send, h_recv, a_send, a1_recv, a2_recv,
    s_send, s_recv, r_send, r_recv, f_send, f_recv, g_send, g_recv, l_send, l_recv,
):
    me = lax.axis_index("ctx")
    xme = lax.axis_index("head")
    src_b, src_j = me // NB, lax.rem(me, NB)
    b = 2 * (me // 16) + lax.rem(me, 2)
    h = lax.rem(me, 16) // 2
    first_block = b == 0

    def ctx(i):
        return {"ctx": i}

    y, z, c = me // 16, h, lax.rem(me, 2)
    k_in, v_in, q_in, t_in = (xs.at[a] for a in range(4))
    loads = [pltpu.make_async_copy(src, xin.at[a], in_sem.at[a]) for a, src in enumerate((k_hbm, v_hbm, q_hbm, t_hbm))]
    weights = [
        pltpu.make_async_copy(wq_hbm, wq_ref, w_sem.at[0]),
        pltpu.make_async_copy(wk_hbm, wk_ref, w_sem.at[1]),
    ]

    bar = pltpu.get_barrier_semaphore()

    def greet(device):
        pl.semaphore_signal(bar, inc=1, device_id=device, device_id_type=MESH)

    for o in FAR:
        for d in range(2):
            if o or d:
                greet(ctx(16 * y + 2 * lax.rem(z + o, NB) + lax.rem(c + d, 2)))
    for o in range(1, 4):
        for d in range(2):
            greet(ctx(16 * lax.rem(y + o, 4) + 2 * z + d))
        greet({"head": lax.rem(xme + o, 4)})
    for load in loads + weights:
        load.start()
    for a in range(4):
        loads[a].wait()
        xs[a] = jnp.swapaxes(xin[a], 0, 1)
    for load in weights:
        load.wait()
    pl.semaphore_wait(bar, 24)

    arrays = ((k_in, kbuf, WIN), (v_in, vbuf, WIN), (q_in, qbuf, 0), (t_in, tbuf, 0))

    def exchange(a, o, act):
        src, dst, base = arrays[a]
        hd = lax.rem(h + o, NB)
        to = place(src_b, hd)
        rows = dst.at[pl.ds(pl.multiple_of(base + CH * src_j, WIN), CH)]

        def remote():
            act(pltpu.make_async_remote_copy(
                src.at[hd], rows, x_send, x_recv.at[a], device_id=ctx(to), device_id_type=MESH))

        if o == 0:
            pl.when(to != me)(remote)
            if act is go:
                @pl.when(to == me)
                def _():
                    pltpu.make_async_copy(src.at[hd], rows, x_recv.at[a]).start()
        else:
            remote()

    def left(ref, sem):
        pltpu.make_async_copy(ref, ref, sem).wait()

    def go(c):
        c.start()

    def sent(c):
        c.wait_send()

    def halo(a, act):
        dst = arrays[a][1]

        @pl.when(b < NB - 1)
        def _():
            act(pltpu.make_async_remote_copy(
                dst.at[pl.ds(NB * CH, WIN)], dst.at[pl.ds(0, WIN)], h_send.at[a], h_recv.at[a],
                device_id=ctx(place(b + 1, h)), device_id_type=MESH))

    for a in range(4):
        for o in FAR:
            exchange(a, o, go)

    @pl.when(first_block)
    def _():
        kbuf[pl.ds(0, WIN)] = jnp.zeros((WIN, HD), BF)
        vbuf[pl.ds(0, WIN)] = jnp.zeros((WIN, HD), BF)

    ci = lax.broadcasted_iota(jnp.int32, (CH + WIN, CH), 0)
    ii = lax.broadcasted_iota(jnp.int32, (CH + WIN, CH), 1)
    inwin = jnp.logical_and(ci > ii, ci <= ii + WIN)
    mask[0] = jnp.where(jnp.logical_and(inwin, jnp.logical_or(ci >= WIN, b > 0)), 0.0, -jnp.inf)
    mask[1] = jnp.where(inwin, 0.0, -jnp.inf)
    eye = jnp.where(
        lax.broadcasted_iota(jnp.int32, (CH, CH), 0) == lax.broadcasted_iota(jnp.int32, (CH, CH), 1),
        1.0, 0.0).astype(BF)
    one_row = jnp.where(lax.broadcasted_iota(jnp.int32, (AUG - HD, CH), 0) < 2, 1.0, 0.0)
    wq1, wk1 = wq_ref[h], wk_ref[h]
    w2q = jnp.concatenate([wq1, -wq1], axis=0)
    w2k = jnp.concatenate([wk1, -wk1], axis=0)

    def arrived(a):
        src, dst, base = arrays[a]
        part = dst.at[pl.ds(base, NB * CH)]
        pltpu.make_async_copy(part, part, x_recv.at[a]).wait()

    arrived(0)
    halo(0, go)

    cidx = lax.broadcasted_iota(jnp.int32, (CH, CH), 0)
    iidx = lax.broadcasted_iota(jnp.int32, (CH, CH), 1)
    lower = cidx <= iidx

    def edges(buf):
        return jnp.concatenate([buf[pl.ds(WIN, WIN)], buf[pl.ds(NB * CH, WIN)]], axis=0)

    def key_chunk(n):
        f = halves(nt(w2k, kbuf[pl.ds(n * CH, CH)]))
        if n == 0:
            bad = jnp.logical_and(first_block, iidx < WIN)
            f = jnp.where(bad, 0.0, f)
        fkt[n] = f
        fkb[n] = nt(eye, f.astype(BF)).astype(BF)

    for n in range(1, NB):
        key_chunk(n)
    fkx = nt(eye, halves(nt(w2k, edges(kbuf))).astype(BF)).astype(BF)
    arrived(1)
    halo(1, go)

    def value_chunk(n):
        va = jnp.concatenate([nt(eye, vbuf[pl.ds(n * CH, CH)]), one_row], axis=0).astype(BF)
        vta[n] = va
        return nn(va, fkb[n])

    vax = jnp.concatenate([nt(eye, edges(vbuf)), one_row], axis=0).astype(BF)
    head_sum = nn(vax[:, :WIN], fkx[:WIN])
    run = head_sum
    for n in range(1, NB):
        pre[n] = run
        run = run + value_chunk(n)
    own1[...] = split(run + nn(vax[:, WIN:], fkx[WIN:]))
    vta[NB, :, pl.ds(0, WIN)] = jnp.concatenate(
        [nt(eye, vbuf[pl.ds(NB * CH, WIN)]), one_row[:, :WIN]], axis=0).astype(BF)

    def scan_copy(o, own, got, recv):
        return pltpu.make_async_remote_copy(
            own, got.at[b], a_send, recv, device_id=ctx(place(lax.rem(b + o, NB), h)),
            device_id_type=MESH)

    def forward(o, act):
        @pl.when(b + o < NB)
        def _():
            act(scan_copy(o, own1, ag1, a1_recv))

    def backward(o, act):
        @pl.when(b - o >= 0)
        def _():
            act(scan_copy(NB - o, own2, ag2, a2_recv))

    for o in range(7, 0, -1):
        forward(o, go)

    @pl.when(b > 0)
    def _():
        for a in range(2):
            part = arrays[a][1].at[pl.ds(0, WIN)]
            pltpu.make_async_copy(part, part, h_recv.at[a]).wait()

    key_chunk(0)
    pre[0] = head_sum - value_chunk(0)

    arrived(2)
    scale = 1.0 / HD**0.5

    def query_chunk(n):
        q = qbuf[pl.ds(n * CH, CH)]
        f = halves(nt(w2q, q))
        fqt[n] = f
        fb = f.astype(BF)
        fqb[n] = fb
        sc = nt(kbuf[pl.ds(n * CH, CH + WIN)], q) * scale
        sc = sc + mask[1 if n else 0]
        top = jnp.max(sc, axis=0, keepdims=True)
        w = jnp.exp(sc - top).astype(BF)
        wn = nn(vta[n], w[:CH]) + nn(vta[n + 1, :, pl.ds(0, WIN)], w[CH:])
        ws = jnp.exp(jnp.minimum(top, 0.0))
        ls = jnp.exp(-jnp.maximum(top, 0.0))
        if n == 0:
            early = jnp.logical_and(first_block, lax.broadcasted_iota(jnp.int32, (1, CH), 1) < WIN)
            ws = jnp.where(early, 1.0, ws)
            ls = jnp.where(early, 0.0, ls)
        am = jnp.where(lower, nn(fkb[n], fb), 0.0).astype(BF)
        ln = nn(vta[n], am) + nn(split(pre[n]), fb)
        win[n] = ws * wn + ls * ln
        scal[n] = jnp.broadcast_to(ls, (8, CH))

    each(query_chunk)

    lin[...] = jnp.zeros((AUG, CH), F32)
    for k in range(1, NB):
        @pl.when(b == k)
        def _():
            left(ag1.at[pl.ds(0, k)], a1_recv)

    for m in range(NB - 1):
        @pl.when(m < b)
        def _():
            lin[...] += ag1[m].astype(F32)
    carry = joined(lin[...])
    carry_b = split(carry)

    def out_chunk(n):
        full = win[n] + scal[n][:1] * nn(carry_b, fqb[n])
        inv = 1.0 / full[HD : HD + 1]
        out = full[:HD] * inv
        outs[n] = out
        scal[n] = jnp.broadcast_to(scal[n][:1] * inv, (8, CH))

    each(out_chunk)
    arrived(3)
    parts = []

    def diff_chunk(n):
        coef, out = scal[n][:1], outs[n]
        diff = out - nt(eye, tbuf[pl.ds(n * CH, CH)])
        g = diff * (2.0 / HD)
        gd = -coef * jnp.sum(g * out, axis=0, keepdims=True)
        scal[n] = jnp.broadcast_to(gd, (8, CH))
        diffs[n] = diff
        ga = jnp.concatenate([coef * g, gd * one_row], axis=0).astype(BF)
        gna[n] = ga
        parts.append(ga)

    each(diff_chunk)
    queries_all = jnp.concatenate([fqb[n] for n in range(NB)], axis=1)
    own2[...] = split(nt(jnp.concatenate(parts, axis=1), queries_all))
    for o in range(7, 0, -1):
        backward(o, go)
    errors = []
    for n in range(NB):
        sq = diffs[n] * diffs[n]
        for r in range(HD // 8):
            errors.append(sq[8 * r : 8 * r + 8])
    while len(errors) > 1:
        errors = [sum(errors[i : i + 2]) for i in range(0, len(errors), 2)]
    la[b] = errors[0]

    def loss_a(o, act):
        act(pltpu.make_async_remote_copy(
            la.at[b], la.at[b], l_send, l_recv.at[0],
            device_id=ctx(place(lax.rem(b + o, NB), h)), device_id_type=MESH))

    def loss_b(o, act):
        act(pltpu.make_async_remote_copy(
            lb.at[xme], lb.at[xme], l_send, l_recv.at[1],
            device_id={"head": lax.rem(xme + o, 4)}, device_id_type=MESH))

    def loss_c(o, act):
        act(pltpu.make_async_remote_copy(
            lc, loss_out.at[h], l_send, l_recv.at[2],
            device_id=ctx(place(b, lax.rem(h + o, NB))), device_id_type=MESH))

    def total(ref, count, level):
        part = ref.at[pl.ds(0, count - 1)]
        pltpu.make_async_copy(part, part, l_recv.at[level]).wait()
        acc = ref[0]
        for m in range(1, count):
            acc = acc + ref[m]
        return acc

    for o in range(1, NB):
        loss_a(o, go)

    def student(j, act):
        to = NB * b + j

        def remote():
            act(pltpu.make_async_remote_copy(
                stu.at[j], stu_got.at[h], s_send, s_recv, device_id=ctx(to), device_id_type=MESH))

        pl.when(to != me)(remote)
        if act is go:
            @pl.when(to == me)
            def _():
                pltpu.make_async_copy(stu.at[j], stu_got.at[h], s_recv).start()

    for j in range(NB):
        stu[j] = nt(eye, outs[j].astype(BF)).astype(BF)
    for j in range(NB):
        student(j, go)

    dq = []

    def mix_chunk(n):
        gd = scal[n][:1]
        ga = gna[n]
        mx = nn(vbuf[pl.ds(n * CH, CH)], ga[:HD]) + gd
        mx = jnp.where(lower, mx, 0.0).astype(BF)
        st = nt(eye, split(pre[n] + carry)).astype(BF)
        gq = nn(fkt[n].astype(BF), mx) + nn(st, ga)
        dq.append(proj_grad(fqt[n], gq))
        lt = nt(eye, split(later[n])).astype(BF)
        gfk[n] = nt(fqb[n], mx) + nn(lt, vta[n])

    suffix = jnp.zeros((AUG, CH), F32)
    for n in reversed(range(NB)):
        later[n] = suffix
        suffix = suffix + nt(gna[n], fqb[n])
    each(mix_chunk)
    gpart[0] = nn(jnp.concatenate(dq, axis=1), qbuf[...]).astype(BF)

    def half(core):
        return pl.ds(pl.multiple_of(HF // 2 * core, HF // 2), HF // 2)

    def share(w, o, act):
        m = lax.rem(b + o, NB)
        act(pltpu.make_async_remote_copy(
            gpart.at[w, half(lax.rem(m, 2))], gsum.at[w, b], r_send, r_recv.at[w],
            device_id=ctx(place(m, h)), device_id_type=MESH))

    def summed(w):
        gsum[w, b] = gpart[w, half(c)]
        part = gsum.at[w, pl.ds(0, NB - 1)]
        pltpu.make_async_copy(part, part, r_recv.at[w]).wait()
        acc = gsum[w, 0].astype(F32)
        for m in range(1, NB):
            acc = acc + gsum[w, m].astype(F32)
        fin[w] = acc.astype(BF)

    def spread(w, o, act):
        act(pltpu.make_async_remote_copy(
            fin.at[w], fin_out.at[w, h, half(c)], f_send, f_recv.at[w, o],
            device_id=ctx(place(b, lax.rem(h + o, NB))), device_id_type=MESH))

    def partner(w, src, head):
        pltpu.make_async_remote_copy(
            src, fin_out.at[w, head, half(c)], g_send, g_recv,
            device_id=ctx(me + 1 - 2 * c), device_id_type=MESH).start()

    def spread_all(w):
        for o in FAR[:-1]:
            spread(w, o, go)
        pltpu.make_async_copy(fin.at[w], fin_out.at[w, h, half(c)], f_recv.at[w, 0]).start()
        partner(w, fin.at[w], h)

    def pass_on(w):
        for o in reversed(FAR[:-1]):
            head = lax.rem(h - o + NB, NB)
            mine = fin_out.at[w, head, half(c)]
            pltpu.make_async_copy(mine, mine, f_recv.at[w, o]).wait()
            partner(w, mine, head)

    for o in range(1, NB):
        share(0, o, go)
    lb[xme] = total(la, NB, 0)
    for o in range(1, 4):
        loss_b(o, go)

    lin[...] = jnp.zeros((AUG, CH), F32)
    for k in range(1, NB):
        @pl.when(b == NB - 1 - k)
        def _():
            left(ag2.at[pl.ds(NB - k, k)], a2_recv)

    for m in range(1, NB):
        @pl.when(m > b)
        def _():
            lin[...] += ag2[m].astype(F32)
    after = nt(eye, split(joined(lin[...]))).astype(BF)
    dk = []

    def key_grad(n):
        dk.append(proj_grad(fkt[n], gfk[n] + nn(after, vta[n])))

    each(key_grad)
    gpart[1] = nn(jnp.concatenate(dk, axis=1), kbuf[pl.ds(0, NB * CH)]).astype(BF)
    for o in range(1, NB):
        share(1, o, go)
    summed(0)
    spread_all(0)
    summed(1)
    spread_all(1)
    lc[...] = total(lb, 4, 1)
    for o in range(1, NB):
        loss_c(o, go)
    pltpu.make_async_copy(lc, loss_out.at[h], l_recv.at[2]).start()

    pltpu.make_async_copy(stu_got, stu_got, s_recv).wait()
    stu_t[...] = jnp.swapaxes(stu_got[...], 0, 1)
    put = pltpu.make_async_copy(stu_t, stu_out, out_sem)
    put.start()
    pass_on(0)
    pass_on(1)

    own = (me == place(src_b, h)).astype(jnp.int32)
    for n in range(2):
        @pl.when(own == n)
        def _():
            left(xs.at[:, pl.ds(0, NB - n)], x_send)
            left(stu.at[pl.ds(0, NB - n)], s_send)

    for a in range(2):
        halo(a, sent)
    left(ag1.at[pl.ds(0, NB - 1)], a_send)
    left(win.at[0, pl.ds(0, 8 * 17)], l_send)
    left(gsum.at[:, pl.ds(0, NB - 1)], r_send)
    left(gsum.at[:, pl.ds(0, NB - 1)], f_send)
    put.wait()
    left(loss_out, l_recv.at[2])
    for w in range(2):
        left(fin.at[w], f_recv.at[w, 0])
    left(gsum, g_send)
    left(gsum, g_recv)


def finish(stu_in, fin_in, loss_in, stu_out, gq_out, gk_out, loss_out, fin, gq, gk, parts, loss, in_sem, out_sem):
    loads = [
        pltpu.make_async_copy(src, dst, in_sem.at[i])
        for i, (src, dst) in enumerate(((fin_in.at[0], fin.at[0]), (fin_in.at[1], fin.at[1]), (loss_in, parts)))
    ]
    stores = [
        pltpu.make_async_copy(src, dst, out_sem.at[i])
        for i, (src, dst) in enumerate(((gq, gq_out), (gk, gk_out), (loss, loss_out), (stu_in, stu_out)))
    ]
    for load in loads:
        load.start()
    stores[3].start()
    loads[0].wait()
    gq[...] = fin[0].astype(F32)
    stores[0].start()
    loads[1].wait()
    gk[...] = fin[1].astype(F32)
    stores[1].start()
    loads[2].wait()
    loss[...] = jnp.sum(parts[...], keepdims=True)[0] * (1.0 / (8192 * 32 * 128))
    stores[2].start()
    for store in stores:
        store.wait()


def per_device(queries, keys, values, teacher, wq, wk):
    anywhere = pl.BlockSpec(memory_space=pl.ANY)
    dma = pltpu.SemaphoreType.DMA
    stu, fin, loss = pl.pallas_call(
        kernel,
        out_shape=(
            jax.ShapeDtypeStruct((CH, NB, HD), BF),
            jax.ShapeDtypeStruct((2, NB, HF, HD), BF),
            jax.ShapeDtypeStruct((NB, 8, CH), F32),
        ),
        in_specs=[anywhere] * 6,
        out_specs=(anywhere,) * 3,
        scratch_shapes=[
            pltpu.VMEM((4, CH, NB, HD), BF),
            pltpu.VMEM((4, NB, CH, HD), BF),
            pltpu.VMEM((NB, HF, HD), BF),
            pltpu.VMEM((NB, HF, HD), BF),
            pltpu.VMEM((NB * CH + WIN, HD), BF),
            pltpu.VMEM((NB * CH + WIN, HD), BF),
            pltpu.VMEM((NB * CH, HD), BF),
            pltpu.VMEM((NB * CH, HD), BF),
            pltpu.VMEM((NB, CH, CH), F32),
            pltpu.VMEM((NB, CH, CH), BF),
            pltpu.VMEM((NB, CH, CH), F32),
            pltpu.VMEM((NB, CH, CH), BF),
            pltpu.VMEM((NB + 1, AUG, CH), BF),
            pltpu.VMEM((NB, AUG, CH), F32),
            pltpu.VMEM((NB, AUG, CH), F32),
            pltpu.VMEM((NB, HD, CH), F32),
            pltpu.VMEM((NB, HD, CH), F32),
            pltpu.VMEM((AUG, CH), F32),
            pltpu.VMEM((NB, AUG, CH), BF),
            pltpu.VMEM((NB, CH, CH), F32),
            pltpu.VMEM((NB, AUG, CH), F32),
            pltpu.VMEM((AUG, CH), BF),
            pltpu.VMEM((NB, AUG, CH), BF),
            pltpu.VMEM((AUG, CH), BF),
            pltpu.VMEM((NB, AUG, CH), BF),
            pltpu.VMEM((NB, CH, HD), BF),
            pltpu.VMEM((NB, CH, HD), BF),
            pltpu.VMEM((CH, NB, HD), BF),
            pltpu.VMEM((2, HF, HD), BF),
            pltpu.VMEM((2, NB, HF // 2, HD), BF),
            pltpu.VMEM((2, HF // 2, HD), BF),
            pltpu.VMEM((NB, 8, CH), F32),
            pltpu.VMEM((4, 8, CH), F32),
            pltpu.VMEM((8, CH), F32),
            pltpu.VMEM((NB, 8, CH), F32),
            pltpu.VMEM((2, CH + WIN, CH), F32),
            dma((4,)), dma((2,)), dma,
            dma, dma((4,)),
            dma((2,)), dma((2,)),
            dma, dma, dma,
            dma, dma,
            dma, dma((2,)),
            dma, dma((2, NB)),
            dma, dma,
            dma, dma((3,)),
        ],
        compiler_params=pltpu.CompilerParams(
            collective_id=0, has_side_effects=True, vmem_limit_bytes=24 * 2**20),
    )(*(pltpu.with_memory_space_constraint(x, pltpu.HBM) for x in (queries, keys, values, teacher, wq, wk)))
    stu, gq, gk, loss = pl.pallas_call(
        finish,
        out_shape=(
            jax.ShapeDtypeStruct((CH, NB, HD), BF),
            jax.ShapeDtypeStruct((NB, HF, HD), F32),
            jax.ShapeDtypeStruct((NB, HF, HD), F32),
            jax.ShapeDtypeStruct((1, 1), F32),
        ),
        in_specs=[anywhere] * 3,
        out_specs=(anywhere,) * 4,
        scratch_shapes=[
            pltpu.VMEM((2, NB, HF, HD), BF),
            pltpu.VMEM((NB, HF, HD), F32),
            pltpu.VMEM((NB, HF, HD), F32),
            pltpu.VMEM((NB, 8, CH), F32),
            pltpu.VMEM((1, 1), F32),
            dma((3,)),
            dma((4,)),
        ],
        compiler_params=pltpu.CompilerParams(vmem_limit_bytes=8 * 2**20),
    )(stu, fin, loss)
    return stu, loss[0, 0], gq, gk


def solution(mesh):
    tok = P("ctx", "head", None)
    par = P("head", None, None)
    return jax.shard_map(
        per_device,
        mesh=mesh,
        in_specs=(tok, tok, tok, tok, par, par),
        out_specs=(tok, P(), par, par),
        check_vma=False,
    )
```

```python
import jax
import jax.numpy as jnp
from jax import lax
from jax.experimental import pallas as pl
from jax.experimental.pallas import tpu as pltpu
from jax.sharding import PartitionSpec as P

NB = 8
CH = 128
WIN = 64
HD = 128
HF = 64
AUG = 144
FAR = (4, 3, 5, 2, 6, 1, 7, 0)
MESH = pl.DeviceIdType.MESH
BF = jnp.bfloat16
F32 = jnp.float32


def nt(a, b):
    return lax.dot_general(a, b, (((1,), (1,)), ((), ())), preferred_element_type=F32)


def nn(a, b):
    return jnp.dot(a, b, preferred_element_type=F32)


def halves(proj):
    e = []
    for s in (proj[:HF], proj[HF:]):
        w = jnp.exp(s - jnp.max(s, axis=0, keepdims=True))
        e.append(w * (1.0 / jnp.sum(w, axis=0, keepdims=True)))
    return jnp.concatenate(e, axis=0)


def proj_grad(feat, grad):
    d = []
    for a in (0, HF):
        u, g = feat[a : a + HF], grad[a : a + HF]
        d.append(u * (g - jnp.sum(u * g, axis=0, keepdims=True)))
    return (d[0] - d[1]).astype(BF)


def split(x):
    norm = x[HD : HD + 1]
    high = norm.astype(BF).astype(F32)
    row = lax.broadcasted_iota(jnp.int32, (AUG - HD, CH), 0)
    aug = jnp.where(row == 0, high, jnp.where(row == 1, norm - high, 0.0))
    return jnp.concatenate([x[:HD], aug], axis=0).astype(BF)


def joined(x):
    return jnp.concatenate([x[:HD], x[HD : HD + 8] + pltpu.roll(x[HD : HD + 8], 7, 0), x[HD + 8 :]], axis=0)


def place(block, head):
    return 16 * (block // 2) + 2 * head + lax.rem(block, 2)


def each(body):
    for n in range(NB):
        body(n)


def kernel(
    q_hbm, k_hbm, v_hbm, t_hbm, wq_hbm, wk_hbm,
    stu_out, fin_out, loss_out,
    xin, xs, wq_ref, wk_ref,
    kbuf, vbuf, qbuf, tbuf, fkt, fkb, fqt, fqb, vta, pre, win, outs, diffs, lin, gna, gfk, later,
    own1, ag1, own2, ag2, stu, stu_got, stu_t, gpart, gsum, fin, la, lb, lc, scal, mask,
    in_sem, w_sem, out_sem,
    x_send, x_recv, h_send, h_recv, a_send, a1_recv, a2_recv,
    s_send, s_recv, r_send, r_recv, f_send, f_recv, g_send, g_recv, l_send, l_recv,
):
    me = lax.axis_index("ctx")
    xme = lax.axis_index("head")
    src_b, src_j = me // NB, lax.rem(me, NB)
    b = 2 * (me // 16) + lax.rem(me, 2)
    h = lax.rem(me, 16) // 2
    first_block = b == 0

    def ctx(i):
        return {"ctx": i}

    y, z, c = me // 16, h, lax.rem(me, 2)
    k_in, v_in, q_in, t_in = (xs.at[a] for a in range(4))
    loads = [pltpu.make_async_copy(src, xin.at[a], in_sem.at[a]) for a, src in enumerate((k_hbm, v_hbm, q_hbm, t_hbm))]
    weights = [
        pltpu.make_async_copy(wq_hbm, wq_ref, w_sem.at[0]),
        pltpu.make_async_copy(wk_hbm, wk_ref, w_sem.at[1]),
    ]

    bar = pltpu.get_barrier_semaphore()

    def greet(device):
        pl.semaphore_signal(bar, inc=1, device_id=device, device_id_type=MESH)

    for o in FAR:
        for d in range(2):
            if o or d:
                greet(ctx(16 * y + 2 * lax.rem(z + o, NB) + lax.rem(c + d, 2)))
    for o in range(1, 4):
        for d in range(2):
            greet(ctx(16 * lax.rem(y + o, 4) + 2 * z + d))
        greet({"head": lax.rem(xme + o, 4)})
    for load in loads + weights:
        load.start()
    for a in range(4):
        loads[a].wait()
        xs[a] = jnp.swapaxes(xin[a], 0, 1)
    for load in weights:
        load.wait()
    pl.semaphore_wait(bar, 24)

    arrays = ((k_in, kbuf, WIN), (v_in, vbuf, WIN), (q_in, qbuf, 0), (t_in, tbuf, 0))

    def exchange(a, o, act):
        src, dst, base = arrays[a]
        hd = lax.rem(h + o, NB)
        to = place(src_b, hd)
        rows = dst.at[pl.ds(pl.multiple_of(base + CH * src_j, WIN), CH)]

        def remote():
            act(pltpu.make_async_remote_copy(
                src.at[hd], rows, x_send, x_recv.at[a], device_id=ctx(to), device_id_type=MESH))

        if o == 0:
            pl.when(to != me)(remote)
            if act is go:
                @pl.when(to == me)
                def _():
                    pltpu.make_async_copy(src.at[hd], rows, x_recv.at[a]).start()
        else:
            remote()

    def left(ref, sem):
        pltpu.make_async_copy(ref, ref, sem).wait()

    def go(c):
        c.start()

    def sent(c):
        c.wait_send()

    def halo(a, act):
        dst = arrays[a][1]

        @pl.when(b < NB - 1)
        def _():
            act(pltpu.make_async_remote_copy(
                dst.at[pl.ds(NB * CH, WIN)], dst.at[pl.ds(0, WIN)], h_send.at[a], h_recv.at[a],
                device_id=ctx(place(b + 1, h)), device_id_type=MESH))

    for a in range(4):
        for o in FAR:
            exchange(a, o, go)

    @pl.when(first_block)
    def _():
        kbuf[pl.ds(0, WIN)] = jnp.zeros((WIN, HD), BF)
        vbuf[pl.ds(0, WIN)] = jnp.zeros((WIN, HD), BF)

    ci = lax.broadcasted_iota(jnp.int32, (CH + WIN, CH), 0)
    ii = lax.broadcasted_iota(jnp.int32, (CH + WIN, CH), 1)
    inwin = jnp.logical_and(ci > ii, ci <= ii + WIN)
    mask[0] = jnp.where(jnp.logical_and(inwin, jnp.logical_or(ci >= WIN, b > 0)), 0.0, -jnp.inf)
    mask[1] = jnp.where(inwin, 0.0, -jnp.inf)
    eye = jnp.where(
        lax.broadcasted_iota(jnp.int32, (CH, CH), 0) == lax.broadcasted_iota(jnp.int32, (CH, CH), 1),
        1.0, 0.0).astype(BF)
    one_row = jnp.where(lax.broadcasted_iota(jnp.int32, (AUG - HD, CH), 0) < 2, 1.0, 0.0)
    wq1, wk1 = wq_ref[h], wk_ref[h]
    w2q = jnp.concatenate([wq1, -wq1], axis=0)
    w2k = jnp.concatenate([wk1, -wk1], axis=0)

    def arrived(a):
        src, dst, base = arrays[a]
        part = dst.at[pl.ds(base, NB * CH)]
        pltpu.make_async_copy(part, part, x_recv.at[a]).wait()

    arrived(0)
    halo(0, go)

    cidx = lax.broadcasted_iota(jnp.int32, (CH, CH), 0)
    iidx = lax.broadcasted_iota(jnp.int32, (CH, CH), 1)
    lower = cidx <= iidx

    def edges(buf):
        return jnp.concatenate([buf[pl.ds(WIN, WIN)], buf[pl.ds(NB * CH, WIN)]], axis=0)

    def key_chunk(n):
        f = halves(nt(w2k, kbuf[pl.ds(n * CH, CH)]))
        if n == 0:
            bad = jnp.logical_and(first_block, iidx < WIN)
            f = jnp.where(bad, 0.0, f)
        fkt[n] = f
        fkb[n] = nt(eye, f.astype(BF)).astype(BF)

    for n in range(1, NB):
        key_chunk(n)
    fkx = nt(eye, halves(nt(w2k, edges(kbuf))).astype(BF)).astype(BF)
    arrived(1)
    halo(1, go)

    def value_chunk(n):
        va = jnp.concatenate([nt(eye, vbuf[pl.ds(n * CH, CH)]), one_row], axis=0).astype(BF)
        vta[n] = va
        return nn(va, fkb[n])

    vax = jnp.concatenate([nt(eye, edges(vbuf)), one_row], axis=0).astype(BF)
    head_sum = nn(vax[:, :WIN], fkx[:WIN])
    run = head_sum
    for n in range(1, NB):
        pre[n] = run
        run = run + value_chunk(n)
    own1[...] = split(run + nn(vax[:, WIN:], fkx[WIN:]))
    vta[NB, :, pl.ds(0, WIN)] = jnp.concatenate(
        [nt(eye, vbuf[pl.ds(NB * CH, WIN)]), one_row[:, :WIN]], axis=0).astype(BF)

    def scan_copy(o, own, got, recv):
        return pltpu.make_async_remote_copy(
            own, got.at[b], a_send, recv, device_id=ctx(place(lax.rem(b + o, NB), h)),
            device_id_type=MESH)

    def forward(o, act):
        @pl.when(b + o < NB)
        def _():
            act(scan_copy(o, own1, ag1, a1_recv))

    def backward(o, act):
        @pl.when(b - o >= 0)
        def _():
            act(scan_copy(NB - o, own2, ag2, a2_recv))

    for o in range(7, 0, -1):
        forward(o, go)

    @pl.when(b > 0)
    def _():
        for a in range(2):
            part = arrays[a][1].at[pl.ds(0, WIN)]
            pltpu.make_async_copy(part, part, h_recv.at[a]).wait()

    key_chunk(0)
    pre[0] = head_sum - value_chunk(0)

    arrived(2)
    scale = 1.0 / HD**0.5

    def query_chunk(n):
        q = qbuf[pl.ds(n * CH, CH)]
        f = halves(nt(w2q, q))
        fqt[n] = f
        fb = f.astype(BF)
        fqb[n] = fb
        sc = nt(kbuf[pl.ds(n * CH, CH + WIN)], q) * scale
        sc = sc + mask[1 if n else 0]
        top = jnp.max(sc, axis=0, keepdims=True)
        w = jnp.exp(sc - top).astype(BF)
        wn = nn(vta[n], w[:CH]) + nn(vta[n + 1, :, pl.ds(0, WIN)], w[CH:])
        ws = jnp.exp(jnp.minimum(top, 0.0))
        ls = jnp.exp(-jnp.maximum(top, 0.0))
        if n == 0:
            early = jnp.logical_and(first_block, lax.broadcasted_iota(jnp.int32, (1, CH), 1) < WIN)
            ws = jnp.where(early, 1.0, ws)
            ls = jnp.where(early, 0.0, ls)
        am = jnp.where(lower, nn(fkb[n], fb), 0.0).astype(BF)
        ln = nn(vta[n], am) + nn(split(pre[n]), fb)
        win[n] = ws * wn + ls * ln
        scal[n] = jnp.broadcast_to(ls, (8, CH))

    each(query_chunk)

    lin[...] = jnp.zeros((AUG, CH), F32)
    for k in range(1, NB):
        @pl.when(b == k)
        def _():
            left(ag1.at[pl.ds(0, k)], a1_recv)

    for m in range(NB - 1):
        @pl.when(m < b)
        def _():
            lin[...] += ag1[m].astype(F32)
    carry = joined(lin[...])
    carry_b = split(carry)

    def out_chunk(n):
        full = win[n] + scal[n][:1] * nn(carry_b, fqb[n])
        inv = 1.0 / full[HD : HD + 1]
        out = full[:HD] * inv
        outs[n] = out
        scal[n] = jnp.broadcast_to(scal[n][:1] * inv, (8, CH))

    each(out_chunk)
    arrived(3)
    parts = []

    def diff_chunk(n):
        coef, out = scal[n][:1], outs[n]
        diff = out - nt(eye, tbuf[pl.ds(n * CH, CH)])
        g = diff * (2.0 / HD)
        gd = -coef * jnp.sum(g * out, axis=0, keepdims=True)
        scal[n] = jnp.broadcast_to(gd, (8, CH))
        diffs[n] = diff
        ga = jnp.concatenate([coef * g, gd * one_row], axis=0).astype(BF)
        gna[n] = ga
        parts.append(ga)

    each(diff_chunk)
    queries_all = jnp.concatenate([fqb[n] for n in range(NB)], axis=1)
    own2[...] = split(nt(jnp.concatenate(parts, axis=1), queries_all))
    for o in range(1, NB):
        backward(o, go)
    errors = []
    for n in range(NB):
        sq = diffs[n] * diffs[n]
        for r in range(HD // 8):
            errors.append(sq[8 * r : 8 * r + 8])
    while len(errors) > 1:
        errors = [sum(errors[i : i + 2]) for i in range(0, len(errors), 2)]
    la[b] = errors[0]

    def loss_a(o, act):
        act(pltpu.make_async_remote_copy(
            la.at[b], la.at[b], l_send, l_recv.at[0],
            device_id=ctx(place(lax.rem(b + o, NB), h)), device_id_type=MESH))

    def loss_b(o, act):
        act(pltpu.make_async_remote_copy(
            lb.at[xme], lb.at[xme], l_send, l_recv.at[1],
            device_id={"head": lax.rem(xme + o, 4)}, device_id_type=MESH))

    def loss_c(o, act):
        act(pltpu.make_async_remote_copy(
            lc, loss_out.at[h], l_send, l_recv.at[2],
            device_id=ctx(place(b, lax.rem(h + o, NB))), device_id_type=MESH))

    def total(ref, count, level):
        part = ref.at[pl.ds(0, count - 1)]
        pltpu.make_async_copy(part, part, l_recv.at[level]).wait()
        acc = ref[0]
        for m in range(1, count):
            acc = acc + ref[m]
        return acc

    for o in range(1, NB):
        loss_a(o, go)

    def student(j, act):
        to = NB * b + j

        def remote():
            act(pltpu.make_async_remote_copy(
                stu.at[j], stu_got.at[h], s_send, s_recv, device_id=ctx(to), device_id_type=MESH))

        pl.when(to != me)(remote)
        if act is go:
            @pl.when(to == me)
            def _():
                pltpu.make_async_copy(stu.at[j], stu_got.at[h], s_recv).start()

    for j in range(NB):
        stu[j] = nt(eye, outs[j].astype(BF)).astype(BF)
    for j in range(NB):
        student(j, go)

    dq = []

    def mix_chunk(n):
        gd = scal[n][:1]
        ga = gna[n]
        mx = nn(vbuf[pl.ds(n * CH, CH)], ga[:HD]) + gd
        mx = jnp.where(lower, mx, 0.0).astype(BF)
        st = nt(eye, split(pre[n] + carry)).astype(BF)
        gq = nn(fkt[n].astype(BF), mx) + nn(st, ga)
        dq.append(proj_grad(fqt[n], gq))
        lt = nt(eye, split(later[n])).astype(BF)
        gfk[n] = nt(fqb[n], mx) + nn(lt, vta[n])

    suffix = jnp.zeros((AUG, CH), F32)
    for n in reversed(range(NB)):
        later[n] = suffix
        suffix = suffix + nt(gna[n], fqb[n])
    each(mix_chunk)
    gpart[0] = nn(jnp.concatenate(dq, axis=1), qbuf[...]).astype(BF)

    def half(core):
        return pl.ds(pl.multiple_of(HF // 2 * core, HF // 2), HF // 2)

    def share(w, o, act):
        m = lax.rem(b + o, NB)
        act(pltpu.make_async_remote_copy(
            gpart.at[w, half(lax.rem(m, 2))], gsum.at[w, b], r_send, r_recv.at[w],
            device_id=ctx(place(m, h)), device_id_type=MESH))

    def summed(w):
        gsum[w, b] = gpart[w, half(c)]
        part = gsum.at[w, pl.ds(0, NB - 1)]
        pltpu.make_async_copy(part, part, r_recv.at[w]).wait()
        acc = gsum[w, 0].astype(F32)
        for m in range(1, NB):
            acc = acc + gsum[w, m].astype(F32)
        fin[w] = acc.astype(BF)

    def spread(w, o, act):
        act(pltpu.make_async_remote_copy(
            fin.at[w], fin_out.at[w, h, half(c)], f_send, f_recv.at[w, o],
            device_id=ctx(place(b, lax.rem(h + o, NB))), device_id_type=MESH))

    def partner(w, src, head):
        pltpu.make_async_remote_copy(
            src, fin_out.at[w, head, half(c)], g_send, g_recv,
            device_id=ctx(me + 1 - 2 * c), device_id_type=MESH).start()

    def spread_all(w):
        for o in FAR[:-1]:
            spread(w, o, go)
        pltpu.make_async_copy(fin.at[w], fin_out.at[w, h, half(c)], f_recv.at[w, 0]).start()
        partner(w, fin.at[w], h)

    def pass_on(w):
        for o in reversed(FAR[:-1]):
            head = lax.rem(h - o + NB, NB)
            mine = fin_out.at[w, head, half(c)]
            pltpu.make_async_copy(mine, mine, f_recv.at[w, o]).wait()
            partner(w, mine, head)

    for o in range(1, NB):
        share(0, o, go)
    lb[xme] = total(la, NB, 0)
    for o in range(1, 4):
        loss_b(o, go)

    lin[...] = jnp.zeros((AUG, CH), F32)
    for k in range(1, NB):
        @pl.when(b == NB - 1 - k)
        def _():
            left(ag2.at[pl.ds(NB - k, k)], a2_recv)

    for m in range(1, NB):
        @pl.when(m > b)
        def _():
            lin[...] += ag2[m].astype(F32)
    after = nt(eye, split(joined(lin[...]))).astype(BF)
    dk = []

    def key_grad(n):
        dk.append(proj_grad(fkt[n], gfk[n] + nn(after, vta[n])))

    each(key_grad)
    gpart[1] = nn(jnp.concatenate(dk, axis=1), kbuf[pl.ds(0, NB * CH)]).astype(BF)
    for o in range(1, NB):
        share(1, o, go)
    summed(0)
    spread_all(0)
    summed(1)
    spread_all(1)
    lc[...] = total(lb, 4, 1)
    for o in range(1, NB):
        loss_c(o, go)
    pltpu.make_async_copy(lc, loss_out.at[h], l_recv.at[2]).start()

    pltpu.make_async_copy(stu_got, stu_got, s_recv).wait()
    stu_t[...] = jnp.swapaxes(stu_got[...], 0, 1)
    put = pltpu.make_async_copy(stu_t, stu_out, out_sem)
    put.start()
    pass_on(0)
    pass_on(1)

    own = (me == place(src_b, h)).astype(jnp.int32)
    for n in range(2):
        @pl.when(own == n)
        def _():
            left(xs.at[:, pl.ds(0, NB - n)], x_send)
            left(stu.at[pl.ds(0, NB - n)], s_send)

    for a in range(2):
        halo(a, sent)
    left(ag1.at[pl.ds(0, NB - 1)], a_send)
    left(win.at[0, pl.ds(0, 8 * 17)], l_send)
    left(gsum.at[:, pl.ds(0, NB - 1)], r_send)
    left(gsum.at[:, pl.ds(0, NB - 1)], f_send)
    put.wait()
    left(loss_out, l_recv.at[2])
    for w in range(2):
        left(fin.at[w], f_recv.at[w, 0])
    left(gsum, g_send)
    left(gsum, g_recv)


def finish(stu_in, fin_in, loss_in, stu_out, gq_out, gk_out, loss_out, fin, gq, gk, parts, loss, in_sem, out_sem):
    loads = [
        pltpu.make_async_copy(src, dst, in_sem.at[i])
        for i, (src, dst) in enumerate(((fin_in.at[0], fin.at[0]), (fin_in.at[1], fin.at[1]), (loss_in, parts)))
    ]
    stores = [
        pltpu.make_async_copy(src, dst, out_sem.at[i])
        for i, (src, dst) in enumerate(((gq, gq_out), (gk, gk_out), (loss, loss_out), (stu_in, stu_out)))
    ]
    for load in loads:
        load.start()
    stores[3].start()
    loads[0].wait()
    gq[...] = fin[0].astype(F32)
    stores[0].start()
    loads[1].wait()
    gk[...] = fin[1].astype(F32)
    stores[1].start()
    loads[2].wait()
    loss[...] = jnp.sum(parts[...], keepdims=True)[0] * (1.0 / (8192 * 32 * 128))
    stores[2].start()
    for store in stores:
        store.wait()


def per_device(queries, keys, values, teacher, wq, wk):
    anywhere = pl.BlockSpec(memory_space=pl.ANY)
    dma = pltpu.SemaphoreType.DMA
    stu, fin, loss = pl.pallas_call(
        kernel,
        out_shape=(
            jax.ShapeDtypeStruct((CH, NB, HD), BF),
            jax.ShapeDtypeStruct((2, NB, HF, HD), BF),
            jax.ShapeDtypeStruct((NB, 8, CH), F32),
        ),
        in_specs=[anywhere] * 6,
        out_specs=(anywhere,) * 3,
        scratch_shapes=[
            pltpu.VMEM((4, CH, NB, HD), BF),
            pltpu.VMEM((4, NB, CH, HD), BF),
            pltpu.VMEM((NB, HF, HD), BF),
            pltpu.VMEM((NB, HF, HD), BF),
            pltpu.VMEM((NB * CH + WIN, HD), BF),
            pltpu.VMEM((NB * CH + WIN, HD), BF),
            pltpu.VMEM((NB * CH, HD), BF),
            pltpu.VMEM((NB * CH, HD), BF),
            pltpu.VMEM((NB, CH, CH), F32),
            pltpu.VMEM((NB, CH, CH), BF),
            pltpu.VMEM((NB, CH, CH), F32),
            pltpu.VMEM((NB, CH, CH), BF),
            pltpu.VMEM((NB + 1, AUG, CH), BF),
            pltpu.VMEM((NB, AUG, CH), F32),
            pltpu.VMEM((NB, AUG, CH), F32),
            pltpu.VMEM((NB, HD, CH), F32),
            pltpu.VMEM((NB, HD, CH), F32),
            pltpu.VMEM((AUG, CH), F32),
            pltpu.VMEM((NB, AUG, CH), BF),
            pltpu.VMEM((NB, CH, CH), F32),
            pltpu.VMEM((NB, AUG, CH), F32),
            pltpu.VMEM((AUG, CH), BF),
            pltpu.VMEM((NB, AUG, CH), BF),
            pltpu.VMEM((AUG, CH), BF),
            pltpu.VMEM((NB, AUG, CH), BF),
            pltpu.VMEM((NB, CH, HD), BF),
            pltpu.VMEM((NB, CH, HD), BF),
            pltpu.VMEM((CH, NB, HD), BF),
            pltpu.VMEM((2, HF, HD), BF),
            pltpu.VMEM((2, NB, HF // 2, HD), BF),
            pltpu.VMEM((2, HF // 2, HD), BF),
            pltpu.VMEM((NB, 8, CH), F32),
            pltpu.VMEM((4, 8, CH), F32),
            pltpu.VMEM((8, CH), F32),
            pltpu.VMEM((NB, 8, CH), F32),
            pltpu.VMEM((2, CH + WIN, CH), F32),
            dma((4,)), dma((2,)), dma,
            dma, dma((4,)),
            dma((2,)), dma((2,)),
            dma, dma, dma,
            dma, dma,
            dma, dma((2,)),
            dma, dma((2, NB)),
            dma, dma,
            dma, dma((3,)),
        ],
        compiler_params=pltpu.CompilerParams(
            collective_id=0, has_side_effects=True, vmem_limit_bytes=24 * 2**20),
    )(*(pltpu.with_memory_space_constraint(x, pltpu.HBM) for x in (queries, keys, values, teacher, wq, wk)))
    stu, gq, gk, loss = pl.pallas_call(
        finish,
        out_shape=(
            jax.ShapeDtypeStruct((CH, NB, HD), BF),
            jax.ShapeDtypeStruct((NB, HF, HD), F32),
            jax.ShapeDtypeStruct((NB, HF, HD), F32),
            jax.ShapeDtypeStruct((1, 1), F32),
        ),
        in_specs=[anywhere] * 3,
        out_specs=(anywhere,) * 4,
        scratch_shapes=[
            pltpu.VMEM((2, NB, HF, HD), BF),
            pltpu.VMEM((NB, HF, HD), F32),
            pltpu.VMEM((NB, HF, HD), F32),
            pltpu.VMEM((NB, 8, CH), F32),
            pltpu.VMEM((1, 1), F32),
            dma((3,)),
            dma((4,)),
        ],
        compiler_params=pltpu.CompilerParams(vmem_limit_bytes=8 * 2**20),
    )(stu, fin, loss)
    return stu, loss[0, 0], gq, gk


def solution(mesh):
    tok = P("ctx", "head", None)
    par = P("head", None, None)
    return jax.shard_map(
        per_device,
        mesh=mesh,
        in_specs=(tok, tok, tok, tok, par, par),
        out_specs=(tok, P(), par, par),
        check_vma=False,
    )
```
